32 devices in a mesh: grp: 2 (over y), tr: 8 (over z, x), root: 2 (over core).
Axes of the slice: x: 2, y: 2, z: 4, core: 2. Of those that a mesh axis runs over, the one named last changes fastest.
Arguments:
- residual: bfloat16 [128, 65536], P('root', ('grp', 'tr')), parts along dimension 1, may hold values from -8 to 8
- subspace: bfloat16 [512, 65536], P(None, ('grp', 'tr')), parts along dimension 1, may hold values from -1 to 1, as said below
- inverses: bfloat16 [16, 512, 512], P(('grp', 'tr')), parts along dimension 0, may hold values from -1 to 3, as said below
- owner_offset: int32 [128], P(('grp', 'tr')), parts along dimension 0, may hold values from 0 to 3, as said below
- listed: int32 [128], P(('grp', 'tr')), parts along dimension 0, may hold values from 0 to 1, as said below
Outputs:
- corrections: float32 [128, 65536], P('root', ('grp', 'tr')), parts along dimension 1
The draws below stay inside these ranges and needn't reach their ends.
There are 2 independent parts, one for each index of `grp`. The reference program is written for one: setup_inputs(seed, part) draws one part's arguments, and reference() takes and returns one part's arrays. A program takes and returns all parts, laid end to end along the dimension named above; each array names one. Nothing has to cross between parts.
Inputs may be any that keep to these rules, and one draw needn't show every extreme that they name: Each entry of subspace lies within the stated range; rows are not normalized. `inverses`: each inverse is a dense real matrix. `owner_offset`: among the 8 blocks of each shard, at least one is listed and has offset 3. Each shard has at least one listed block and at least one unlisted block.
All inputs are finite; a program needn't handle non-finite values.
Results may differ from the reference program's by a relative error of at most 0.0065.
Values may be sent and summed in bfloat16 or wider, within the bound.
A program may use at most 64 MiB of HBM per device.

```python
import math
import jax
import jax.numpy as jnp
from jax import lax

BLK = 512
R = 128
S = 512
OFFS = 4
PASSES = 2
BLK_DEV = 8
NB = 64
NT = 32768
PAIRS = 8


def subspace_values(key):
    base = jax.random.fold_in(key, 11)
    row_key, common_key, mix_key, scale_key = jax.random.split(base, 4)
    position = jnp.arange(NT, dtype=jnp.float32) / NT
    rows = jax.random.truncated_normal(row_key, -4.0, 4.0, (S, NT), jnp.float32)
    common = jax.random.truncated_normal(common_key, -4.0, 4.0, (8, NT), jnp.float32)
    mixing = jax.random.truncated_normal(mix_key, -4.0, 4.0, (S, 8), jnp.float32) * math.sqrt(0.6 / S)
    scales = jnp.exp(jax.random.uniform(scale_key, (S,), jnp.float32, math.log(0.6), math.log(1.25)))
    envelope = jnp.exp(0.5 * math.log(3.0) * position)
    envelope = envelope / jnp.sqrt(jnp.mean(envelope * envelope))
    entries = rows + jnp.dot(mixing, common, precision=lax.Precision.HIGHEST)
    return entries * envelope[None, :] * scales[:, None] / jnp.sqrt(jnp.float32(NT))


def draw_subspace(key, part):
    return subspace_values(key).astype(jnp.bfloat16)


def draw_residual(key, part):
    basis = subspace_values(key)
    noise_key, weight_key = jax.random.split(jax.random.fold_in(key, 37))
    noise = jax.random.truncated_normal(noise_key, -4.0, 4.0, (R, NT), jnp.float32)
    weights = jax.random.truncated_normal(weight_key, -4.0, 4.0, (R, S), jnp.float32)
    row_norms = jnp.sqrt(jnp.sum(basis * basis, axis=1))
    weights = weights * jnp.sqrt(jnp.float32(NT) / S) / row_norms[None, :]
    values = noise + jnp.dot(weights, basis, precision=lax.Precision.HIGHEST)
    return jnp.clip(values, -8.0, 8.0).astype(jnp.bfloat16)


def draw_inverses(key, part):
    first_key, second_key = jax.random.split(jax.random.fold_in(key, 23))
    diagonal = jnp.exp(jax.random.uniform(first_key, (PAIRS, BLK), jnp.float32, math.log(0.5), math.log(2.0)))
    off_diagonal = jax.random.truncated_normal(second_key, -4.0, 4.0, (PAIRS, BLK, BLK), jnp.float32) * (0.5 / math.sqrt(BLK))
    matrix = off_diagonal + jnp.eye(BLK, dtype=jnp.float32)[None, :, :] * diagonal[:, None, :]
    return matrix.astype(jnp.bfloat16)


def block_plan(key):
    plan_key = jax.random.fold_in(key, 71)
    offset_key, listed_key, forced_key = jax.random.split(plan_key, 3)
    shard_count = NB // BLK_DEV
    offsets = jax.random.randint(offset_key, (NB,), 0, OFFS, dtype=jnp.int32)
    marks = (jax.random.randint(listed_key, (NB,), 0, 8, dtype=jnp.int32) < 7).astype(jnp.int32)
    forced_slot = jax.random.randint(forced_key, (shard_count,), 0, BLK_DEV, dtype=jnp.int32)
    skipped_slot = (forced_slot + 1) % BLK_DEV
    within = jnp.arange(NB, dtype=jnp.int32) % BLK_DEV
    forced = within == jnp.repeat(forced_slot, BLK_DEV)
    skipped = within == jnp.repeat(skipped_slot, BLK_DEV)
    offsets = jnp.where(forced, OFFS - 1, offsets).astype(jnp.int32)
    marks = jnp.where(skipped, 0, marks).astype(jnp.int32)
    marks = jnp.where(forced, 1, marks).astype(jnp.int32)
    return (offsets, marks)


def draw_owner_offset(key, part):
    return block_plan(key)[0]


def draw_listed(key, part):
    return block_plan(key)[1]


def setup_inputs(seed: int = 0, part: int = 0) -> dict:
    splits = jax.random.split(jax.random.key(seed), 6)
    part_keys = jax.random.split(jax.random.fold_in(splits[5], part), 6)
    return {
        "residual": draw_residual(jax.random.fold_in(jax.random.fold_in(splits[5], part), 71), part),
        "subspace": draw_subspace(jax.random.fold_in(jax.random.fold_in(splits[5], part), 71), part),
        "inverses": draw_inverses(jax.random.fold_in(jax.random.fold_in(splits[5], part), 71), part),
        "owner_offset": draw_owner_offset(jax.random.fold_in(jax.random.fold_in(splits[5], part), 71), part),
        "listed": draw_listed(jax.random.fold_in(jax.random.fold_in(splits[5], part), 71), part),
    }


def reference(residual, subspace, inverses, owner_offset, listed):
    block_count = residual.shape[1] // BLK
    blocks = residual.reshape(R, block_count, BLK).transpose(1, 0, 2)
    holder = jnp.arange(block_count, dtype=jnp.int32) // BLK_DEV
    owner_pair = ((holder + owner_offset) % PAIRS).astype(jnp.int32)

    def apply_block(packet):
        residual_block, pair_index, is_listed = packet
        solved = jnp.dot(residual_block, inverses[pair_index], preferred_element_type=jnp.float32)
        return jnp.where(is_listed > 0, solved, residual_block.astype(jnp.float32))

    precond = lax.map(apply_block, (blocks, owner_pair, listed))
    current = precond.transpose(1, 0, 2).reshape(R, block_count * BLK)
    for repeat in range(PASSES):
        rounded = current.astype(jnp.bfloat16)
        correlation = lax.dot_general(rounded, subspace, (((1,), (1,)), ((), ())), preferred_element_type=jnp.float32)
        coefficients = correlation.astype(jnp.bfloat16)
        current = current - jnp.dot(coefficients, subspace, preferred_element_type=jnp.float32)
    return current
```

```python
import functools
import jax
import jax.numpy as jnp
from jax import lax
from jax.experimental import pallas as pl
from jax.experimental.pallas import tpu as pltpu
from jax.sharding import PartitionSpec as P

OFFS = 4
PASSES = 2
LINK = jnp.bfloat16
SUBLANES = 8
CHUNKS = 8
EARLY = 3
MESH = pl.DeviceIdType.MESH
VMEM_GRANT = 61_700_000


def each(count, body):
    if count <= 16:
        for i in range(count):
            body(i)
    else:
        pl.loop(0, count)(body)


def flows(side):
    every, early, late = range(CHUNKS), range(EARLY), range(EARLY, CHUNKS)
    if side == 0:
        own = [(every, 2, "near"), ]
        order = []
        for q in every:
            order.append((2, q, [(1, "twin")]))
            if q in early:
                order.append((1, q, [(3, "near")]))
        order += [(1, q, []) for q in late]
        order += [(3, q, [(2, "twin")]) for q in early]
        order += [(3, q, []) for q in late]
    else:
        own = [(every, 1, "twin"), (late, 2, "near")]
        order = [(2, q, [(3, "twin")]) for q in late]
        order += [(1, q, [(3, "near")]) for q in every]
        order += [(2, q, []) for q in early]
        order += [(3, q, []) for q in every]
    return own, order


def dot_t(a, b):
    return lax.dot_general(a, b, (((1,), (1,)), ((), ())), preferred_element_type=jnp.float32)


def kernel(n, roots, off, listed, res, sub, inv, work, sub_v, coef, table, res_v, gram_sum, gram_hi, gram_lo, corr,
           partial, inbox, slabs, load_sem, hop_send, hop_recv, swap_send, swap_recv,
           rs_send, rs_recv, ag_send, ag_recv):
    me = lax.axis_index("tr")
    root = lax.axis_index("root")
    rows, cols = res.shape
    blk = inv.shape[1]
    spans = sub.shape[0]
    blocks = cols // blk
    share = blk // roots
    owners = slabs.shape[1]
    base = (n - owners) // 2
    slab = rows // owners
    chunk = share // CHUNKS

    def block(b):
        return pl.ds(b * blk, blk)

    own_load = pltpu.make_async_copy(inv.at[0], table.at[0], load_sem.at[0])
    res_load = pltpu.make_async_copy(res, res_v, load_sem.at[1])
    sub_load = pltpu.make_async_copy(sub, sub_v, load_sem.at[2])
    sub_load.start()
    own_load.start()
    res_load.start()

    def is_owner(device):
        return jnp.logical_and(device >= base, device < base + owners)

    side = lax.rem(me, 2)
    twin = me + 1 - 2 * side
    peers = {"twin": twin, "near": lax.rem(me + n - 2, n)}

    barrier = pltpu.get_barrier_semaphore()

    def linked(d):
        peer = lax.rem(me + d + 1, n)
        close = jnp.logical_or(jnp.logical_or(d + 1 == 2, d + 1 == n - 2), peer == twin)
        return jnp.logical_or(close, jnp.logical_or(is_owner(me), is_owner(peer)))

    def greet(d):
        def signal():
            pl.semaphore_signal(barrier, inc=1, device_id={"tr": lax.rem(me + d + 1, n)}, device_id_type=MESH)

        pl.when(linked(d))(signal)

    for d in range(1, roots):
        pl.semaphore_signal(barrier, inc=1, device_id={"root": lax.rem(root + d, roots)}, device_id_type=MESH)
    each(n - 1, greet)
    partners = lax.fori_loop(0, n - 1, lambda d, c: c + linked(d).astype(jnp.int32), jnp.int32(roots - 1))
    pl.semaphore_wait(barrier, partners)

    def chunk_rows(half, q):
        return pl.ds(pl.multiple_of(half * share + q * chunk, chunk), chunk)

    def hop(src, q, slot, peer, sem):
        return pltpu.make_async_remote_copy(
            src_ref=src, dst_ref=table.at[slot, chunk_rows(root, q)],
            send_sem=hop_send.at[sem, q], recv_sem=hop_recv.at[slot, q],
            device_id={"tr": peers[peer]}, device_id_type=MESH)

    def own_hop(q, slot, peer, sem):
        return hop(inv.at[0, chunk_rows(root, q)], q, slot, peer, sem)

    def relay(e, q, slot, peer, sem):
        return hop(table.at[e, chunk_rows(root, q)], q, slot, peer, sem)

    def swap(e, q, half):
        rows_q = table.at[e, chunk_rows(half, q)]
        return pltpu.make_async_remote_copy(
            src_ref=rows_q, dst_ref=rows_q,
            send_sem=swap_send.at[e, q], recv_sem=swap_recv.at[e, q],
            device_id={"root": 1 - root}, device_id_type=MESH)

    def gram(b):
        part = dot_t(sub_v[:, block(b)], sub_v[:, block(b)])
        gram_sum[...] = part if b == 0 else gram_sum[...] + part

    def exchange(s):
        own, order = flows(s)
        steps = list(range(blocks))
        for j, (chunks, slot, peer) in enumerate(own):
            for q in chunks:
                own_hop(q, slot, peer, j).start()
        sub_load.wait()
        for i, (e, q, targets) in enumerate(order):
            if i % 2 == 0 and steps:
                gram(steps.pop(0))
            relay(e, q, e, "twin", 0).wait_recv()
            for slot, peer in targets:
                relay(e, q, slot, peer, 1 + e).start()
            swap(e, q, root).start()
        for b in steps:
            gram(b)

    def close(s):
        own, order = flows(s)
        for j, (chunks, slot, peer) in enumerate(own):
            for q in chunks:
                own_hop(q, slot, peer, j).wait_send()
        for e, q, targets in order:
            for slot, peer in targets:
                relay(e, q, slot, peer, 1 + e).wait_send()
            swap(e, q, root).wait_send()

    for s in range(2):
        pl.when(side == s)(functools.partial(exchange, s))
    high = gram_sum[...].astype(jnp.bfloat16)
    gram_hi[...] = high
    gram_lo[...] = (gram_sum[...] - high.astype(jnp.float32)).astype(jnp.bfloat16)
    own_load.wait()
    res_load.wait()
    for e in range(1, OFFS):
        for q in range(CHUNKS):
            swap(e, q, 1 - root).wait_recv()

    total = jnp.zeros((rows, spans), jnp.float32)
    for b in range(blocks):
        x = res_v[:, block(b)]
        solved = jnp.dot(x, table[off[b]], preferred_element_type=jnp.float32)
        kept = jnp.where(listed[b] > 0, solved, x.astype(jnp.float32))
        work[:, block(b)] = kept
        total += dot_t(kept.astype(jnp.bfloat16), sub_v[:, block(b)])
    corr[...] = total

    def rs_copy(i, j):
        return pltpu.make_async_remote_copy(
            src_ref=partial.at[i, j], dst_ref=inbox.at[i, me],
            send_sem=rs_send.at[i, j], recv_sem=rs_recv.at[i, me],
            device_id={"tr": base + j}, device_id_type=MESH)

    def rs_in(i, peer):
        return pltpu.make_async_remote_copy(
            src_ref=inbox.at[i, peer], dst_ref=inbox.at[i, peer],
            send_sem=rs_send.at[i, 0], recv_sem=rs_recv.at[i, peer],
            device_id={"tr": peer}, device_id_type=MESH)

    def ag_copy(i, d):
        return pltpu.make_async_remote_copy(
            src_ref=slabs.at[i, me - base], dst_ref=slabs.at[i, me - base],
            send_sem=ag_send.at[i, d], recv_sem=ag_recv.at[i, me - base],
            device_id={"tr": lax.rem(me + d + 1, n)}, device_id_type=MESH)

    def ag_in(i, j):
        return pltpu.make_async_remote_copy(
            src_ref=slabs.at[i, j], dst_ref=slabs.at[i, j],
            send_sem=ag_send.at[i, 0], recv_sem=ag_recv.at[i, j],
            device_id={"tr": base + j}, device_id_type=MESH)

    def for_other_owners(body):
        for j in range(owners):
            pl.when(me != base + j)(functools.partial(body, j))

    def own_sum(i):
        inbox[i, me] = partial[i, me - base]
        each(n - 1, lambda d: rs_in(i, lax.rem(me + d + 1, n)).wait_recv())
        slabs[i, me - base] = jnp.sum(inbox[i].astype(jnp.float32), axis=0).astype(jnp.bfloat16)
        each(n - 1, lambda d: ag_copy(i, d).start())

    def reduce(i, total, cover):
        partial[i] = total.reshape(owners, slab, spans).astype(partial.dtype)
        for_other_owners(lambda j: rs_copy(i, j).start())
        pl.when(is_owner(me))(functools.partial(own_sum, i))
        cover()
        for_other_owners(lambda j: ag_in(i, j).wait_recv())
        return jnp.concatenate(
            [slabs[i, j].astype(jnp.float32) for j in range(owners)], axis=0).astype(jnp.bfloat16)

    first = reduce(0, total, lambda: None)
    total = corr[...] - (
        jnp.dot(first, gram_hi[...], preferred_element_type=jnp.float32)
        + jnp.dot(first, gram_lo[...], preferred_element_type=jnp.float32))

    def update():
        for b in range(blocks):
            work[:, block(b)] -= jnp.dot(first, sub_v[:, block(b)], preferred_element_type=jnp.float32)

    coef[...] = reduce(1, total, update)

    for s in range(2):
        pl.when(side == s)(functools.partial(close, s))
    for i in range(PASSES):
        for_other_owners(lambda j: rs_copy(i, j).wait_send())

        def sent():
            each(n - 1, lambda d: ag_copy(i, d).wait_send())

        pl.when(is_owner(me))(sent)


def finish(blk, work, sub_v, coef, out, out_v, out_sem):
    blocks = work.shape[1] // blk

    def store(b):
        cols = pl.ds(b * blk, blk)
        return pltpu.make_async_copy(out_v.at[:, cols], out.at[:, cols], out_sem.at[b])

    for b in range(blocks):
        cols = pl.ds(b * blk, blk)
        out_v[:, cols] = work[:, cols] - jnp.dot(coef[...], sub_v[:, cols], preferred_element_type=jnp.float32)
        store(b).start()
    for b in range(blocks):
        store(b).wait()


def per_device(n, roots, residual, subspace, inverses, owner_offset, listed):
    rows, cols = residual.shape
    spans = subspace.shape[0]
    blk = inverses.shape[1]
    blocks = cols // blk
    owners = min(n // 2, rows // SUBLANES)
    slab = rows // owners
    hbm = pl.BlockSpec(memory_space=pl.ANY)
    smem = pl.BlockSpec(memory_space=pltpu.SMEM)
    vmem = pl.BlockSpec(memory_space=pltpu.VMEM)
    dma = pltpu.SemaphoreType.DMA
    held = pl.pallas_call(
        functools.partial(kernel, n, roots),
        out_shape=(
            pltpu.VMEM((rows, cols), jnp.float32),
            pltpu.VMEM((spans, cols), jnp.bfloat16),
            pltpu.VMEM((rows, spans), jnp.bfloat16),
        ),
        in_specs=[smem, smem, hbm, hbm, hbm],
        out_specs=(vmem, vmem, vmem),
        scratch_shapes=[
            pltpu.VMEM((OFFS, blk, blk), jnp.bfloat16),
            pltpu.VMEM((rows, cols), jnp.bfloat16),
            pltpu.VMEM((spans, spans), jnp.float32),
            pltpu.VMEM((spans, spans), jnp.bfloat16),
            pltpu.VMEM((spans, spans), jnp.bfloat16),
            pltpu.VMEM((rows, spans), jnp.float32),
            pltpu.VMEM((PASSES, owners, slab, spans), LINK),
            pltpu.VMEM((PASSES, n, slab, spans), LINK),
            pltpu.VMEM((PASSES, owners, slab, spans), jnp.bfloat16),
            dma((3,)),
            dma((1 + OFFS, CHUNKS)), dma((OFFS, CHUNKS)),
            dma((OFFS, CHUNKS)), dma((OFFS, CHUNKS)),
            dma((PASSES, owners)), dma((PASSES, n)),
            dma((PASSES, n)), dma((PASSES, owners)),
        ],
        compiler_params=pltpu.CompilerParams(
            collective_id=0, has_side_effects=True, vmem_limit_bytes=VMEM_GRANT),
    )(owner_offset, listed, residual, subspace, inverses)
    return pl.pallas_call(
        functools.partial(finish, blk),
        out_shape=jax.ShapeDtypeStruct((rows, cols), jnp.float32),
        in_specs=[vmem, vmem, vmem],
        out_specs=hbm,
        scratch_shapes=[pltpu.VMEM((rows, cols), jnp.float32), dma((blocks,))],
        compiler_params=pltpu.CompilerParams(vmem_limit_bytes=16 * 2**20),
    )(*held)


def solution(mesh):
    body = functools.partial(per_device, mesh.shape["tr"], mesh.shape["root"])
    return jax.shard_map(
        body,
        mesh=mesh,
        in_specs=(
            P("root", ("grp", "tr")),
            P(None, ("grp", "tr")),
            P(("grp", "tr"), None, None),
            P(("grp", "tr")),
            P(("grp", "tr")),
        ),
        out_specs=P("root", ("grp", "tr")),
        check_vma=False,
    )
```

```python
import functools
import jax
import jax.numpy as jnp
from jax import lax
from jax.experimental import pallas as pl
from jax.experimental.pallas import tpu as pltpu
from jax.sharding import PartitionSpec as P

OFFS = 4
PASSES = 2
LINK = jnp.bfloat16
SUBLANES = 8
LANES = 128
CHUNKS = 8
EARLY = 3
TREE_AT = 19
TWINS_AT = 26
MESH = pl.DeviceIdType.MESH
VMEM_GRANT = 61_700_000


def each(count, body):
    if count <= 16:
        for i in range(count):
            body(i)
    else:
        pl.loop(0, count)(body)


def flows(side):
    every, early, late = range(CHUNKS), range(EARLY), range(EARLY, CHUNKS)
    if side == 0:
        own = [(every, 2, "near"), ]
        order = []
        for q in every:
            order.append((2, q, [(1, "twin")]))
            if q in early:
                order.append((1, q, [(3, "near")]))
        order += [(1, q, []) for q in late]
        order += [(3, q, [(2, "twin")]) for q in early]
        order += [(3, q, []) for q in late]
    else:
        own = [(every, 1, "twin"), (late, 2, "near")]
        order = [(2, q, [(3, "twin")]) for q in late]
        order += [(1, q, [(3, "near")]) for q in every]
        order += [(2, q, []) for q in early]
        order += [(3, q, []) for q in every]
    return own, order


def dot_t(a, b):
    return lax.dot_general(a, b, (((1,), (1,)), ((), ())), preferred_element_type=jnp.float32)


def kernel(n, roots, off, listed, res, sub, inv, work, sub_v, coef, table, res_v, gram_sum, gram_hi, gram_lo, corr,
           partial, inbox, slabs, strips, diag_out, diag_in, diag, tree_out, tree_in,
           load_sem, hop_send, hop_recv, swap_send, swap_recv, rs_send, rs_recv, ag_send, ag_recv,
           tree_send, tree_recv, diag_send, diag_recv, pair_send, pair_recv):
    me = lax.axis_index("tr")
    root = lax.axis_index("root")
    rows, cols = res.shape
    blk = inv.shape[1]
    spans = sub.shape[0]
    blocks = cols // blk
    share = blk // roots
    owners = slabs.shape[1]
    base = (n - owners) // 2
    width = spans // owners
    chunk = share // CHUNKS
    shared = strips is not None
    half = spans // roots

    def block(b):
        return pl.ds(b * blk, blk)

    own_load = pltpu.make_async_copy(inv.at[0], table.at[0], load_sem.at[0])
    res_load = pltpu.make_async_copy(res, res_v, load_sem.at[1])
    sub_load = pltpu.make_async_copy(sub, sub_v, load_sem.at[2])
    sub_load.start()
    own_load.start()
    res_load.start()

    def is_owner(device):
        return jnp.logical_and(device >= base, device < base + owners)

    side = lax.rem(me, 2)
    twin = me + 1 - 2 * side
    peers = {"twin": twin, "near": lax.rem(me + n - 2, n)}

    barrier = pltpu.get_barrier_semaphore()

    def linked(d):
        peer = lax.rem(me + d + 1, n)
        close = jnp.logical_or(jnp.logical_or(d + 1 == 2, d + 1 == n - 2), peer == twin)
        return jnp.logical_or(close, jnp.logical_or(is_owner(me), is_owner(peer)))

    def greet(d):
        def signal():
            pl.semaphore_signal(barrier, inc=1, device_id={"tr": lax.rem(me + d + 1, n)}, device_id_type=MESH)

        pl.when(linked(d))(signal)

    for d in range(1, roots):
        pl.semaphore_signal(barrier, inc=1, device_id={"root": lax.rem(root + d, roots)}, device_id_type=MESH)
    each(n - 1, greet)
    partners = lax.fori_loop(0, n - 1, lambda d, c: c + linked(d).astype(jnp.int32), jnp.int32(roots - 1))
    pl.semaphore_wait(barrier, partners)

    def chunk_rows(half, q):
        return pl.ds(pl.multiple_of(half * share + q * chunk, chunk), chunk)

    def hop(src, q, slot, peer, sem):
        return pltpu.make_async_remote_copy(
            src_ref=src, dst_ref=table.at[slot, chunk_rows(root, q)],
            send_sem=hop_send.at[sem, q], recv_sem=hop_recv.at[slot, q],
            device_id={"tr": peers[peer]}, device_id_type=MESH)

    def own_hop(q, slot, peer, sem):
        return hop(inv.at[0, chunk_rows(root, q)], q, slot, peer, sem)

    def relay(e, q, slot, peer, sem):
        return hop(table.at[e, chunk_rows(root, q)], q, slot, peer, sem)

    def swap(e, q, half):
        rows_q = table.at[e, chunk_rows(half, q)]
        return pltpu.make_async_remote_copy(
            src_ref=rows_q, dst_ref=rows_q,
            send_sem=swap_send.at[e, q], recv_sem=swap_recv.at[e, q],
            device_id={"root": 1 - root}, device_id_type=MESH)

    def gram_step(b):
        mine = sub_v[pl.ds(pl.multiple_of(root * half, half), half), block(b)] if shared else sub_v[:, block(b)]
        part = dot_t(sub_v[:, block(b)], mine)
        gram_sum[...] = part if b == 0 else gram_sum[...] + part

    lower = me < n // 2
    toward = jnp.where(lower, me + 2, me - 2)

    def strip(k, beside=False):
        owner = (1 - side if beside else side) + 2 * k
        return pl.ds(pl.multiple_of(owner * width, width), width)

    def tree_copy(k, peer):
        return pltpu.make_async_remote_copy(
            src_ref=tree_out.at[k], dst_ref=tree_in.at[k], send_sem=tree_send.at[k], recv_sem=tree_recv.at[k],
            device_id={"tr": peer}, device_id_type=MESH)

    def diag_copy(t):
        return pltpu.make_async_remote_copy(
            src_ref=diag_out.at[t], dst_ref=diag_in.at[me], send_sem=diag_send.at[t], recv_sem=diag_recv.at[me],
            device_id={"tr": base + 2 * root + t}, device_id_type=MESH)

    def diag_from(peer):
        return pltpu.make_async_remote_copy(
            src_ref=diag_out.at[0], dst_ref=diag_in.at[peer], send_sem=diag_send.at[0], recv_sem=diag_recv.at[peer],
            device_id={"tr": peer}, device_id_type=MESH)

    def pair_copy(ref, k):
        return pltpu.make_async_remote_copy(
            src_ref=ref, dst_ref=ref, send_sem=pair_send.at[k], recv_sem=pair_recv.at[k],
            device_id={"root": 1 - root}, device_id_type=MESH)

    def for_own_diag(body):
        for t in range(2):
            pl.when(me != base + 2 * root + t)(functools.partial(body, t))

    def start_tree():
        shape = (width, width)
        on = lax.broadcasted_iota(jnp.int32, shape, 0) == lax.broadcasted_iota(jnp.int32, shape, 1)
        for t in range(2):
            place = pl.ds(pl.multiple_of((2 * root + t) * width, width), width)
            span = pl.ds(t * width, width)
            square = gram_sum[place, span]
            line = jnp.sum(jnp.where(on, square, 0.0), axis=0, keepdims=True)
            diag_out[t] = jnp.broadcast_to(line, diag_out.shape[1:])
            gram_sum[place, span] = jnp.where(on, 0.0, square)
        for k in range(2):
            tree_out[k] = gram_sum[strip(k, beside=True), :].astype(LINK)
            tree_copy(k, twin).start()
        for_own_diag(lambda t: diag_copy(t).start())

    def sum_twins():
        for k in range(2):
            tree_copy(k, twin).wait_recv()
            gram_sum[strip(k), :] += tree_in[k].astype(jnp.float32)

        def outer():
            for k in range(2):
                tree_out[2 + k] = gram_sum[strip(k), :].astype(LINK)
                tree_copy(2 + k, toward).start()

        pl.when(jnp.logical_not(is_owner(me)))(outer)

    def sum_outer():
        for k in range(2):
            tree_copy(2 + k, toward).wait_recv()
            gram_sum[strip(k), :] += tree_in[2 + k].astype(jnp.float32)
        far = pl.ds(pl.multiple_of((side + 2 * lower.astype(jnp.int32)) * width, width), width)
        tree_out[4] = gram_sum[far, :].astype(LINK)
        tree_copy(4, toward).start()

    def sum_inner():
        tree_copy(4, toward).wait_recv()
        near = pl.ds(pl.multiple_of((me - base) * width, width), width)
        strips[root] = (gram_sum[near, :] + tree_in[4].astype(jnp.float32)).astype(LINK)
        pair_copy(strips.at[root], 0).start()

        def sum_diag():
            diag_in[me] = diag_out[lax.rem(me - base, 2)]
            each(n - 1, lambda d: diag_from(lax.rem(me + d + 1, n)).wait_recv())
            diag[...] = jnp.sum(diag_in[...], axis=0)
            pair_copy(diag, 1).start()

        pl.when((me - base) // 2 == root)(sum_diag)

    def paired():
        pair_copy(strips.at[1 - root], 0).wait_recv()
        pl.when((me - base) // 2 != root)(lambda: pair_copy(diag, 1).wait_recv())

    def exchange(s):
        own, order = flows(s)
        for j, (chunks, slot, peer) in enumerate(own):
            for q in chunks:
                own_hop(q, slot, peer, j).start()
        sub_load.wait()
        for i, (e, q, targets) in enumerate(order):
            if i < blocks:
                gram_step(i)
            if shared and i == TREE_AT:
                start_tree()
            if shared and i == TWINS_AT:
                sum_twins()
            relay(e, q, e, "twin", 0).wait_recv()
            for slot, peer in targets:
                relay(e, q, slot, peer, 1 + e).start()
            swap(e, q, root).start()

    def close(s):
        own, order = flows(s)
        for j, (chunks, slot, peer) in enumerate(own):
            for q in chunks:
                own_hop(q, slot, peer, j).wait_send()
        for e, q, targets in order:
            for slot, peer in targets:
                relay(e, q, slot, peer, 1 + e).wait_send()
            swap(e, q, root).wait_send()

    for s in range(2):
        pl.when(side == s)(functools.partial(exchange, s))
    if shared:
        pass
    else:
        high = gram_sum[...].astype(jnp.bfloat16)
        gram_hi[...] = high
        gram_lo[...] = (gram_sum[...] - high.astype(jnp.float32)).astype(jnp.bfloat16)
    own_load.wait()
    res_load.wait()
    for e in range(1, OFFS):
        for q in range(CHUNKS):
            swap(e, q, 1 - root).wait_recv()

    total = jnp.zeros((rows, spans), jnp.float32)
    for b in range(blocks):
        x = res_v[:, block(b)]
        solved = jnp.dot(x, table[off[b]], preferred_element_type=jnp.float32)
        kept = jnp.where(listed[b] > 0, solved, x.astype(jnp.float32))
        work[:, block(b)] = kept
        total += dot_t(kept.astype(jnp.bfloat16), sub_v[:, block(b)])
        if shared and b == TWINS_AT - 3 * CHUNKS:
            sum_twins()

    def rs_copy(i, j):
        return pltpu.make_async_remote_copy(
            src_ref=partial.at[i, j], dst_ref=inbox.at[i, me],
            send_sem=rs_send.at[i, j], recv_sem=rs_recv.at[i, me],
            device_id={"tr": base + j}, device_id_type=MESH)

    def rs_in(i, peer):
        return pltpu.make_async_remote_copy(
            src_ref=inbox.at[i, peer], dst_ref=inbox.at[i, peer],
            send_sem=rs_send.at[i, 0], recv_sem=rs_recv.at[i, peer],
            device_id={"tr": peer}, device_id_type=MESH)

    def ag_copy(i, d):
        return pltpu.make_async_remote_copy(
            src_ref=slabs.at[i, me - base], dst_ref=slabs.at[i, me - base],
            send_sem=ag_send.at[i, d], recv_sem=ag_recv.at[i, me - base],
            device_id={"tr": lax.rem(me + d + 1, n)}, device_id_type=MESH)

    def ag_in(i, j):
        return pltpu.make_async_remote_copy(
            src_ref=slabs.at[i, j], dst_ref=slabs.at[i, j],
            send_sem=ag_send.at[i, 0], recv_sem=ag_recv.at[i, j],
            device_id={"tr": base + j}, device_id_type=MESH)

    def for_other_owners(body):
        for j in range(owners):
            pl.when(me != base + j)(functools.partial(body, j))

    def send_slab(i, value):
        slabs[i, me - base] = value
        each(n - 1, lambda d: ag_copy(i, d).start())

    def own_sum(i):
        if shared:
            sum_outer()
        inbox[i, me] = partial[i, me - base]
        each(n - 1, lambda d: rs_in(i, lax.rem(me + d + 1, n)).wait_recv())
        total = jnp.sum(inbox[i].astype(jnp.float32), axis=0)
        send_slab(i, total.astype(jnp.bfloat16))
        if shared:
            sum_inner()
            arrive(i)
            first = gathered(i)
            paired()
            again = sum(
                dot_t(first[:, h * half:(h + 1) * half], strips[h]) for h in range(roots))
            own = slabs[i, me - base].astype(jnp.float32)
            send_slab(i + 1, (total - (again + own * diag[pl.ds(0, 1), :])).astype(jnp.bfloat16))

    def scatter(i, total):
        for j in range(owners):
            partial[i, j] = total[:, j * width:(j + 1) * width].astype(partial.dtype)
        for_other_owners(lambda j: rs_copy(i, j).start())
        pl.when(is_owner(me))(functools.partial(own_sum, i))

    def arrive(i):
        for_other_owners(lambda j: ag_in(i, j).wait_recv())

    def gathered(i):
        return jnp.concatenate([slabs[i, j] for j in range(owners)], axis=1)

    def update(first):
        for b in range(blocks):
            work[:, block(b)] -= jnp.dot(first, sub_v[:, block(b)], preferred_element_type=jnp.float32)

    if not shared:
        corr[...] = total
    scatter(0, total)
    if shared:
        pl.when(jnp.logical_not(is_owner(me)))(functools.partial(arrive, 0))
    else:
        arrive(0)
    first = gathered(0)
    if not shared:
        scatter(1, corr[...] - (
            jnp.dot(first, gram_hi[...], preferred_element_type=jnp.float32)
            + jnp.dot(first, gram_lo[...], preferred_element_type=jnp.float32)))
    update(first)
    arrive(1)
    coef[...] = gathered(1)

    for s in range(2):
        pl.when(side == s)(functools.partial(close, s))
    for i in range(PASSES):
        if not (shared and i):
            for_other_owners(lambda j: rs_copy(i, j).wait_send())

        def sent():
            each(n - 1, lambda d: ag_copy(i, d).wait_send())

        pl.when(is_owner(me))(sent)
    if shared:
        for k in range(2):
            tree_copy(k, twin).wait_send()
        for_own_diag(lambda t: diag_copy(t).wait_send())

        def inner_sent():
            tree_copy(4, toward).wait_send()
            pair_copy(strips.at[root], 0).wait_send()
            pl.when((me - base) // 2 == root)(lambda: pair_copy(diag, 1).wait_send())

        def outer_sent():
            for k in range(2):
                tree_copy(2 + k, toward).wait_send()

        pl.when(is_owner(me))(inner_sent)
        pl.when(jnp.logical_not(is_owner(me)))(outer_sent)


def finish(blk, work, sub_v, coef, out, out_v, out_sem):
    blocks = work.shape[1] // blk

    def store(b):
        cols = pl.ds(b * blk, blk)
        return pltpu.make_async_copy(out_v.at[:, cols], out.at[:, cols], out_sem.at[b])

    for b in range(blocks):
        cols = pl.ds(b * blk, blk)
        out_v[:, cols] = work[:, cols] - jnp.dot(coef[...], sub_v[:, cols], preferred_element_type=jnp.float32)
        store(b).start()
    for b in range(blocks):
        store(b).wait()


def per_device(n, roots, residual, subspace, inverses, owner_offset, listed):
    rows, cols = residual.shape
    spans = subspace.shape[0]
    blk = inverses.shape[1]
    blocks = cols // blk
    owners = min(n // 2, spans // LANES)
    width = spans // owners
    hbm = pl.BlockSpec(memory_space=pl.ANY)
    smem = pl.BlockSpec(memory_space=pltpu.SMEM)
    vmem = pl.BlockSpec(memory_space=pltpu.VMEM)
    dma = pltpu.SemaphoreType.DMA
    shared = roots == 2 and owners == 4 and n == 2 * owners
    f32, bf16 = jnp.float32, jnp.bfloat16
    if shared:
        gram = {
            "gram_sum": pltpu.VMEM((spans, spans // roots), f32),
            "strips": pltpu.VMEM((roots, width, spans // roots), LINK),
            "diag_out": pltpu.VMEM((2, SUBLANES, width), f32), "diag_in": pltpu.VMEM((n, SUBLANES, width), f32),
            "diag": pltpu.VMEM((SUBLANES, width), f32),
            "tree_out": pltpu.VMEM((5, width, spans // roots), LINK),
            "tree_in": pltpu.VMEM((5, width, spans // roots), LINK),
            "tree_send": dma((5,)), "tree_recv": dma((5,)), "diag_send": dma((2,)), "diag_recv": dma((n,)),
            "pair_send": dma((2,)), "pair_recv": dma((2,)),
        }
        rounds = 1
    else:
        gram = {
            "gram_sum": pltpu.VMEM((spans, spans), f32), "corr": pltpu.VMEM((rows, spans), f32),
            "gram_hi": pltpu.VMEM((spans, spans), bf16), "gram_lo": pltpu.VMEM((spans, spans), bf16),
        }
        rounds = PASSES
    scratch = {
        "table": pltpu.VMEM((OFFS, blk, blk), bf16), "res_v": pltpu.VMEM((rows, cols), bf16),
        "partial": pltpu.VMEM((rounds, owners, rows, width), LINK),
        "inbox": pltpu.VMEM((rounds, n, rows, width), LINK),
        "slabs": pltpu.VMEM((PASSES, owners, rows, width), bf16),
        "load_sem": dma((3,)),
        "hop_send": dma((1 + OFFS, CHUNKS)), "hop_recv": dma((OFFS, CHUNKS)),
        "swap_send": dma((OFFS, CHUNKS)), "swap_recv": dma((OFFS, CHUNKS)),
        "rs_send": dma((rounds, owners)), "rs_recv": dma((rounds, n)),
        "ag_send": dma((PASSES, n)), "ag_recv": dma((PASSES, owners)),
        **gram,
    }
    absent = dict.fromkeys(
        ("gram_hi", "gram_lo", "corr", "strips", "diag_out", "diag_in", "diag", "tree_out", "tree_in",
         "tree_send", "tree_recv", "diag_send", "diag_recv", "pair_send", "pair_recv"))

    def body(off, listed, res, sub, inv, work, sub_v, coef, *refs):
        kernel(n, roots, off, listed, res, sub, inv, work, sub_v, coef, **{**absent, **dict(zip(scratch, refs))})

    held = pl.pallas_call(
        body,
        out_shape=(
            pltpu.VMEM((rows, cols), jnp.float32),
            pltpu.VMEM((spans, cols), jnp.bfloat16),
            pltpu.VMEM((rows, spans), jnp.bfloat16),
        ),
        in_specs=[smem, smem, hbm, hbm, hbm],
        out_specs=(vmem, vmem, vmem),
        scratch_shapes=list(scratch.values()),
        compiler_params=pltpu.CompilerParams(
            collective_id=0, has_side_effects=True, vmem_limit_bytes=VMEM_GRANT),
    )(owner_offset, listed, residual, subspace, inverses)
    return pl.pallas_call(
        functools.partial(finish, blk),
        out_shape=jax.ShapeDtypeStruct((rows, cols), jnp.float32),
        in_specs=[vmem, vmem, vmem],
        out_specs=hbm,
        scratch_shapes=[pltpu.VMEM((rows, cols), jnp.float32), dma((blocks,))],
        compiler_params=pltpu.CompilerParams(vmem_limit_bytes=16 * 2**20),
    )(*held)


def solution(mesh):
    body = functools.partial(per_device, mesh.shape["tr"], mesh.shape["root"])
    return jax.shard_map(
        body,
        mesh=mesh,
        in_specs=(
            P("root", ("grp", "tr")),
            P(None, ("grp", "tr")),
            P(("grp", "tr"), None, None),
            P(("grp", "tr")),
            P(("grp", "tr")),
        ),
        out_specs=P("root", ("grp", "tr")),
        check_vma=False,
    )
```

```python
import functools
import jax
import jax.numpy as jnp
from jax import lax
from jax.experimental import pallas as pl
from jax.experimental.pallas import tpu as pltpu
from jax.sharding import PartitionSpec as P

OFFS = 4
PASSES = 2
LINK = jnp.bfloat16
SUBLANES = 8
LANES = 128
CHUNKS = 8
LOW = 0
BOTH = 4
CROSS = 3
LEAD = 3.5
TREE_AT = 23
TWINS_AT = 32
MESH = pl.DeviceIdType.MESH
VMEM_GRANT = 61_700_000


def each(count, body):
    if count <= 16:
        for i in range(count):
            body(i)
    else:
        pl.loop(0, count)(body)


def flows(side):
    every, low, both, high = range(CHUNKS), range(LOW), range(LOW, LOW + BOTH), range(LOW + BOTH, CHUNKS)
    crossing = range(CHUNKS - CROSS, CHUNKS)
    due = []

    def arrive(start, chunks, slot, *targets):
        for i, q in enumerate(chunks):
            due.append((start + i, slot, q, [(there, peer) for there, peer, among in targets if q in among]))

    if side == 0:
        own = [(every, 2, "near")]
        arrive(0, every, 2, (1, "twin", every), (3, "cross", crossing))
        arrive(0.5, every, 1, (3, "near", range(LOW + BOTH)))
        arrive(CHUNKS, low, 3, (2, "twin", every))
        arrive(CHUNKS, both, 3)
        arrive(CHUNKS, high, 3)
    else:
        own = [(every, 1, "twin"), (high, 2, "near"), (both, 2, "near")]
        arrive(0, high, 2, (3, "twin", every))
        arrive(len(high), both, 2)
        arrive(LEAD, every, 1, (3, "near", range(CHUNKS - CROSS)))
        arrive(CHUNKS + LEAD, low, 2)
        arrive(CHUNKS, range(CHUNKS - CROSS), 3)
        arrive(CHUNKS + 2, crossing, 3)
    due.sort(key=lambda event: event[0])
    return own, [event[1:] for event in due]


def dot_t(a, b):
    return lax.dot_general(a, b, (((1,), (1,)), ((), ())), preferred_element_type=jnp.float32)


def kernel(n, roots, off, listed, res, sub, inv, work, sub_v, coef, table, res_v, gram_sum, gram_hi, gram_lo, corr,
           partial, inbox, slabs, strips, diag_out, diag_in, diag, tree_out, tree_in,
           load_sem, hop_send, hop_recv, swap_send, swap_recv, rs_send, rs_recv, ag_send, ag_recv,
           tree_send, tree_recv, diag_send, diag_recv, pair_send, pair_recv):
    me = lax.axis_index("tr")
    root = lax.axis_index("root")
    rows, cols = res.shape
    blk = inv.shape[1]
    spans = sub.shape[0]
    blocks = cols // blk
    share = blk // roots
    owners = slabs.shape[1]
    base = (n - owners) // 2
    width = spans // owners
    chunk = share // CHUNKS
    shared = strips is not None
    half = spans // roots

    def block(b):
        return pl.ds(b * blk, blk)

    own_load = pltpu.make_async_copy(inv.at[0], table.at[0], load_sem.at[0])
    res_load = pltpu.make_async_copy(res, res_v, load_sem.at[1])
    sub_load = pltpu.make_async_copy(sub, sub_v, load_sem.at[2])
    sub_load.start()
    own_load.start()
    res_load.start()

    def is_owner(device):
        return jnp.logical_and(device >= base, device < base + owners)

    side = lax.rem(me, 2)
    twin = me + 1 - 2 * side
    peers = {"twin": twin, "near": lax.rem(me + n - 2, n), "cross": lax.rem(me + n - 1, n)}

    barrier = pltpu.get_barrier_semaphore()

    def linked(d):
        peer = lax.rem(me + d + 1, n)
        close = jnp.logical_or(jnp.logical_or(d + 1 == 2, d + 1 == n - 2), peer == twin)
        return jnp.logical_or(close, jnp.logical_or(is_owner(me), is_owner(peer)))

    def greet(d):
        def signal():
            pl.semaphore_signal(barrier, inc=1, device_id={"tr": lax.rem(me + d + 1, n)}, device_id_type=MESH)

        pl.when(linked(d))(signal)

    for d in range(1, roots):
        pl.semaphore_signal(barrier, inc=1, device_id={"root": lax.rem(root + d, roots)}, device_id_type=MESH)
    each(n - 1, greet)
    partners = lax.fori_loop(0, n - 1, lambda d, c: c + linked(d).astype(jnp.int32), jnp.int32(roots - 1))
    pl.semaphore_wait(barrier, partners)

    def chunk_rows(half, q):
        return pl.ds(pl.multiple_of(half * share + q * chunk, chunk), chunk)

    def hop(src, q, slot, peer, sem):
        return pltpu.make_async_remote_copy(
            src_ref=src, dst_ref=table.at[slot, chunk_rows(root, q)],
            send_sem=hop_send.at[sem, q], recv_sem=hop_recv.at[slot, q],
            device_id={"tr": peers[peer]}, device_id_type=MESH)

    def own_hop(q, slot, peer, sem):
        return hop(inv.at[0, chunk_rows(root, q)], q, slot, peer, sem)

    def relay(e, q, slot, peer, sem):
        return hop(table.at[e, chunk_rows(root, q)], q, slot, peer, sem)

    def swap(e, q, half):
        rows_q = table.at[e, chunk_rows(half, q)]
        return pltpu.make_async_remote_copy(
            src_ref=rows_q, dst_ref=rows_q,
            send_sem=swap_send.at[e, q], recv_sem=swap_recv.at[e, q],
            device_id={"root": 1 - root}, device_id_type=MESH)

    def gram_step(b):
        mine = sub_v[pl.ds(pl.multiple_of(root * half, half), half), block(b)] if shared else sub_v[:, block(b)]
        part = dot_t(sub_v[:, block(b)], mine)
        gram_sum[...] = part if b == 0 else gram_sum[...] + part

    lower = me < n // 2
    toward = jnp.where(lower, me + 2, me - 2)
    beyond = jnp.where(lower, me + 4, me - 4)

    def strip(k, beside=False):
        owner = (1 - side if beside else side) + 2 * k
        return pl.ds(pl.multiple_of(owner * width, width), width)

    def tree_copy(k, peer):
        return pltpu.make_async_remote_copy(
            src_ref=tree_out.at[k], dst_ref=tree_in.at[k], send_sem=tree_send.at[k], recv_sem=tree_recv.at[k],
            device_id={"tr": peer}, device_id_type=MESH)

    def diag_copy(t):
        return pltpu.make_async_remote_copy(
            src_ref=diag_out.at[t], dst_ref=diag_in.at[me], send_sem=diag_send.at[t], recv_sem=diag_recv.at[me],
            device_id={"tr": base + 2 * root + t}, device_id_type=MESH)

    def diag_from(peer):
        return pltpu.make_async_remote_copy(
            src_ref=diag_out.at[0], dst_ref=diag_in.at[peer], send_sem=diag_send.at[0], recv_sem=diag_recv.at[peer],
            device_id={"tr": peer}, device_id_type=MESH)

    def pair_copy(ref, k):
        return pltpu.make_async_remote_copy(
            src_ref=ref, dst_ref=ref, send_sem=pair_send.at[k], recv_sem=pair_recv.at[k],
            device_id={"root": 1 - root}, device_id_type=MESH)

    def for_own_diag(body):
        for t in range(2):
            pl.when(me != base + 2 * root + t)(functools.partial(body, t))

    def start_tree():
        shape = (width, width)
        on = lax.broadcasted_iota(jnp.int32, shape, 0) == lax.broadcasted_iota(jnp.int32, shape, 1)
        for t in range(2):
            place = pl.ds(pl.multiple_of((2 * root + t) * width, width), width)
            span = pl.ds(t * width, width)
            square = gram_sum[place, span]
            line = jnp.sum(jnp.where(on, square, 0.0), axis=0, keepdims=True)
            diag_out[t] = jnp.broadcast_to(line, diag_out.shape[1:])
            gram_sum[place, span] = jnp.where(on, 0.0, square)
        for k in range(2):
            tree_out[k] = gram_sum[strip(k, beside=True), :].astype(LINK)
            tree_copy(k, twin).start()
        for_own_diag(lambda t: diag_copy(t).start())

    def half_rows(far):
        k = lower.astype(jnp.int32) if far else 1 - lower.astype(jnp.int32)
        return pl.ds(pl.multiple_of((side + 2 * k) * width, width), width)

    def sum_twins():
        for k in range(2):
            tree_copy(k, twin).wait_recv()
            gram_sum[strip(k), :] += tree_in[k].astype(jnp.float32)

        def outer():
            tree_out[3] = gram_sum[half_rows(True), :].astype(LINK)
            tree_copy(3, beyond).start()
            tree_out[2] = gram_sum[half_rows(False), :].astype(LINK)
            tree_copy(2, toward).start()

        def inner():
            tree_out[4] = gram_sum[half_rows(True), :].astype(LINK)
            tree_copy(4, toward).start()

        pl.when(jnp.logical_not(is_owner(me)))(outer)
        pl.when(is_owner(me))(inner)

    def sum_inner():
        total = gram_sum[half_rows(False), :]
        for k in (4, 2, 3):
            tree_copy(k, toward).wait_recv()
            total += tree_in[k].astype(jnp.float32)
        strips[root] = total.astype(LINK)
        pair_copy(strips.at[root], 0).start()

        def sum_diag():
            diag_in[me] = diag_out[lax.rem(me - base, 2)]
            each(n - 1, lambda d: diag_from(lax.rem(me + d + 1, n)).wait_recv())
            diag[...] = jnp.sum(diag_in[...], axis=0)
            pair_copy(diag, 1).start()

        pl.when((me - base) // 2 == root)(sum_diag)

    def paired():
        pair_copy(strips.at[1 - root], 0).wait_recv()
        pl.when((me - base) // 2 != root)(lambda: pair_copy(diag, 1).wait_recv())

    def exchange(s):
        own, order = flows(s)
        for j, (chunks, slot, peer) in enumerate(own):
            for q in chunks:
                own_hop(q, slot, peer, j).start()
        sub_load.wait()
        for i, (e, q, targets) in enumerate(order):
            if i < blocks:
                gram_step(i)
            if shared and i == TREE_AT:
                start_tree()
            if shared and i == TWINS_AT:
                sum_twins()
            relay(e, q, e, "twin", 0).wait_recv()
            for j, (slot, peer) in enumerate(targets):
                relay(e, q, slot, peer, 2 + e if j == 0 else 2 + OFFS).start()
            swap(e, q, root).start()

    def close(s):
        own, order = flows(s)
        for j, (chunks, slot, peer) in enumerate(own):
            for q in chunks:
                own_hop(q, slot, peer, j).wait_send()
        for e, q, targets in order:
            for j, (slot, peer) in enumerate(targets):
                relay(e, q, slot, peer, 2 + e if j == 0 else 2 + OFFS).wait_send()
            swap(e, q, root).wait_send()

    for s in range(2):
        pl.when(side == s)(functools.partial(exchange, s))
    if shared:
        pass
    else:
        high = gram_sum[...].astype(jnp.bfloat16)
        gram_hi[...] = high
        gram_lo[...] = (gram_sum[...] - high.astype(jnp.float32)).astype(jnp.bfloat16)
    own_load.wait()
    res_load.wait()
    for e in range(1, OFFS):
        for q in range(CHUNKS):
            swap(e, q, 1 - root).wait_recv()

    total = jnp.zeros((rows, spans), jnp.float32)
    for b in range(blocks):
        x = res_v[:, block(b)]
        solved = jnp.dot(x, table[off[b]], preferred_element_type=jnp.float32)
        kept = jnp.where(listed[b] > 0, solved, x.astype(jnp.float32))
        work[:, block(b)] = kept
        total += dot_t(kept.astype(jnp.bfloat16), sub_v[:, block(b)])
        if shared and b == TWINS_AT - 3 * CHUNKS:
            sum_twins()

    def rs_copy(i, j):
        return pltpu.make_async_remote_copy(
            src_ref=partial.at[i, j], dst_ref=inbox.at[i, me],
            send_sem=rs_send.at[i, j], recv_sem=rs_recv.at[i, me],
            device_id={"tr": base + j}, device_id_type=MESH)

    def rs_in(i, peer):
        return pltpu.make_async_remote_copy(
            src_ref=inbox.at[i, peer], dst_ref=inbox.at[i, peer],
            send_sem=rs_send.at[i, 0], recv_sem=rs_recv.at[i, peer],
            device_id={"tr": peer}, device_id_type=MESH)

    def ag_copy(i, d):
        return pltpu.make_async_remote_copy(
            src_ref=slabs.at[i, me - base], dst_ref=slabs.at[i, me - base],
            send_sem=ag_send.at[i, d], recv_sem=ag_recv.at[i, me - base],
            device_id={"tr": lax.rem(me + d + 1, n)}, device_id_type=MESH)

    def ag_in(i, j):
        return pltpu.make_async_remote_copy(
            src_ref=slabs.at[i, j], dst_ref=slabs.at[i, j],
            send_sem=ag_send.at[i, 0], recv_sem=ag_recv.at[i, j],
            device_id={"tr": base + j}, device_id_type=MESH)

    def for_other_owners(body):
        for j in range(owners):
            pl.when(me != base + j)(functools.partial(body, j))

    def send_slab(i, value):
        slabs[i, me - base] = value
        each(n - 1, lambda d: ag_copy(i, d).start())

    def own_sum(i):
        inbox[i, me] = partial[i, me - base]
        each(n - 1, lambda d: rs_in(i, lax.rem(me + d + 1, n)).wait_recv())
        total = jnp.sum(inbox[i].astype(jnp.float32), axis=0)
        send_slab(i, total.astype(jnp.bfloat16))
        if shared:
            sum_inner()
            arrive(i)
            first = gathered(i)
            paired()
            again = sum(
                dot_t(first[:, h * half:(h + 1) * half], strips[h]) for h in range(roots))
            own = slabs[i, me - base].astype(jnp.float32)
            send_slab(i + 1, (total - (again + own * diag[pl.ds(0, 1), :])).astype(jnp.bfloat16))

    def scatter(i, total):
        for j in range(owners):
            partial[i, j] = total[:, j * width:(j + 1) * width].astype(partial.dtype)
        for_other_owners(lambda j: rs_copy(i, j).start())
        if shared and TWINS_AT >= 3 * CHUNKS + blocks:
            sum_twins()
        pl.when(is_owner(me))(functools.partial(own_sum, i))

    def arrive(i):
        for_other_owners(lambda j: ag_in(i, j).wait_recv())

    def gathered(i):
        return jnp.concatenate([slabs[i, j] for j in range(owners)], axis=1)

    def update(first):
        for b in range(blocks):
            work[:, block(b)] -= jnp.dot(first, sub_v[:, block(b)], preferred_element_type=jnp.float32)

    if not shared:
        corr[...] = total
    scatter(0, total)
    if shared:
        pl.when(jnp.logical_not(is_owner(me)))(functools.partial(arrive, 0))
    else:
        arrive(0)
    first = gathered(0)
    if not shared:
        scatter(1, corr[...] - (
            jnp.dot(first, gram_hi[...], preferred_element_type=jnp.float32)
            + jnp.dot(first, gram_lo[...], preferred_element_type=jnp.float32)))
    update(first)
    arrive(1)
    coef[...] = gathered(1)

    for s in range(2):
        pl.when(side == s)(functools.partial(close, s))
    for i in range(PASSES):
        if not (shared and i):
            for_other_owners(lambda j: rs_copy(i, j).wait_send())

        def sent():
            each(n - 1, lambda d: ag_copy(i, d).wait_send())

        pl.when(is_owner(me))(sent)
    if shared:
        for k in range(2):
            tree_copy(k, twin).wait_send()
        for_own_diag(lambda t: diag_copy(t).wait_send())

        def inner_sent():
            tree_copy(4, toward).wait_send()
            pair_copy(strips.at[root], 0).wait_send()
            pl.when((me - base) // 2 == root)(lambda: pair_copy(diag, 1).wait_send())

        def outer_sent():
            tree_copy(2, toward).wait_send()
            tree_copy(3, beyond).wait_send()

        pl.when(is_owner(me))(inner_sent)
        pl.when(jnp.logical_not(is_owner(me)))(outer_sent)


def finish(blk, work, sub_v, coef, out, out_v, out_sem):
    blocks = work.shape[1] // blk

    def store(b):
        cols = pl.ds(b * blk, blk)
        return pltpu.make_async_copy(out_v.at[:, cols], out.at[:, cols], out_sem.at[b])

    for b in range(blocks):
        cols = pl.ds(b * blk, blk)
        out_v[:, cols] = work[:, cols] - jnp.dot(coef[...], sub_v[:, cols], preferred_element_type=jnp.float32)
        store(b).start()
    for b in range(blocks):
        store(b).wait()


def per_device(n, roots, residual, subspace, inverses, owner_offset, listed):
    rows, cols = residual.shape
    spans = subspace.shape[0]
    blk = inverses.shape[1]
    blocks = cols // blk
    owners = min(n // 2, spans // LANES)
    width = spans // owners
    hbm = pl.BlockSpec(memory_space=pl.ANY)
    smem = pl.BlockSpec(memory_space=pltpu.SMEM)
    vmem = pl.BlockSpec(memory_space=pltpu.VMEM)
    dma = pltpu.SemaphoreType.DMA
    shared = roots == 2 and owners == 4 and n == 2 * owners
    f32, bf16 = jnp.float32, jnp.bfloat16
    if shared:
        gram = {
            "gram_sum": pltpu.VMEM((spans, spans // roots), f32),
            "strips": pltpu.VMEM((roots, width, spans // roots), LINK),
            "diag_out": pltpu.VMEM((2, SUBLANES, width), f32), "diag_in": pltpu.VMEM((n, SUBLANES, width), f32),
            "diag": pltpu.VMEM((SUBLANES, width), f32),
            "tree_out": pltpu.VMEM((5, width, spans // roots), LINK),
            "tree_in": pltpu.VMEM((5, width, spans // roots), LINK),
            "tree_send": dma((5,)), "tree_recv": dma((5,)), "diag_send": dma((2,)), "diag_recv": dma((n,)),
            "pair_send": dma((2,)), "pair_recv": dma((2,)),
        }
        rounds = 1
    else:
        gram = {
            "gram_sum": pltpu.VMEM((spans, spans), f32), "corr": pltpu.VMEM((rows, spans), f32),
            "gram_hi": pltpu.VMEM((spans, spans), bf16), "gram_lo": pltpu.VMEM((spans, spans), bf16),
        }
        rounds = PASSES
    scratch = {
        "table": pltpu.VMEM((OFFS, blk, blk), bf16), "res_v": pltpu.VMEM((rows, cols), bf16),
        "partial": pltpu.VMEM((rounds, owners, rows, width), LINK),
        "inbox": pltpu.VMEM((rounds, n, rows, width), LINK),
        "slabs": pltpu.VMEM((PASSES, owners, rows, width), bf16),
        "load_sem": dma((3,)),
        "hop_send": dma((OFFS + 3, CHUNKS)), "hop_recv": dma((OFFS, CHUNKS)),
        "swap_send": dma((OFFS, CHUNKS)), "swap_recv": dma((OFFS, CHUNKS)),
        "rs_send": dma((rounds, owners)), "rs_recv": dma((rounds, n)),
        "ag_send": dma((PASSES, n)), "ag_recv": dma((PASSES, owners)),
        **gram,
    }
    absent = dict.fromkeys(
        ("gram_hi", "gram_lo", "corr", "strips", "diag_out", "diag_in", "diag", "tree_out", "tree_in",
         "tree_send", "tree_recv", "diag_send", "diag_recv", "pair_send", "pair_recv"))

    def body(off, listed, res, sub, inv, work, sub_v, coef, *refs):
        kernel(n, roots, off, listed, res, sub, inv, work, sub_v, coef, **{**absent, **dict(zip(scratch, refs))})

    held = pl.pallas_call(
        body,
        out_shape=(
            pltpu.VMEM((rows, cols), jnp.float32),
            pltpu.VMEM((spans, cols), jnp.bfloat16),
            pltpu.VMEM((rows, spans), jnp.bfloat16),
        ),
        in_specs=[smem, smem, hbm, hbm, hbm],
        out_specs=(vmem, vmem, vmem),
        scratch_shapes=list(scratch.values()),
        compiler_params=pltpu.CompilerParams(
            collective_id=0, has_side_effects=True, vmem_limit_bytes=VMEM_GRANT),
    )(owner_offset, listed, residual, subspace, inverses)
    return pl.pallas_call(
        functools.partial(finish, blk),
        out_shape=jax.ShapeDtypeStruct((rows, cols), jnp.float32),
        in_specs=[vmem, vmem, vmem],
        out_specs=hbm,
        scratch_shapes=[pltpu.VMEM((rows, cols), jnp.float32), dma((blocks,))],
        compiler_params=pltpu.CompilerParams(vmem_limit_bytes=16 * 2**20),
    )(*held)


def solution(mesh):
    body = functools.partial(per_device, mesh.shape["tr"], mesh.shape["root"])
    return jax.shard_map(
        body,
        mesh=mesh,
        in_specs=(
            P("root", ("grp", "tr")),
            P(None, ("grp", "tr")),
            P(("grp", "tr"), None, None),
            P(("grp", "tr")),
            P(("grp", "tr")),
        ),
        out_specs=P("root", ("grp", "tr")),
        check_vma=False,
    )
```

```python
import functools
import jax
import jax.numpy as jnp
from jax import lax
from jax.experimental import pallas as pl
from jax.experimental.pallas import tpu as pltpu
from jax.sharding import PartitionSpec as P

OFFS = 4
PASSES = 2
LINK = jnp.bfloat16
SUBLANES = 8
LANES = 128
CHUNKS = 8
LOW = 0
BOTH = 4
CROSS = 3
LEAD = 3.5
TREE_AT = 23
MESH = pl.DeviceIdType.MESH
VMEM_GRANT = 61_700_000


def each(count, body):
    if count <= 16:
        for i in range(count):
            body(i)
    else:
        pl.loop(0, count)(body)


def flows(side):
    every, low, both, high = range(CHUNKS), range(LOW), range(LOW, LOW + BOTH), range(LOW + BOTH, CHUNKS)
    crossing = range(CHUNKS - CROSS, CHUNKS)
    due = []

    def arrive(start, chunks, slot, *targets):
        for i, q in enumerate(chunks):
            due.append((start + i, slot, q, [(there, peer) for there, peer, among in targets if q in among]))

    if side == 0:
        own = [(every, 2, "near")]
        arrive(0, every, 2, (1, "twin", every), (3, "cross", crossing))
        arrive(0.5, every, 1, (3, "near", range(LOW + BOTH)))
        arrive(CHUNKS, low, 3, (2, "twin", every))
        arrive(CHUNKS, both, 3)
        arrive(CHUNKS, high, 3)
    else:
        own = [(every, 1, "twin"), (high, 2, "near"), (both, 2, "near")]
        arrive(0, high, 2, (3, "twin", every))
        arrive(len(high), both, 2)
        arrive(LEAD, every, 1, (3, "near", range(CHUNKS - CROSS)))
        arrive(CHUNKS + LEAD, low, 2)
        arrive(CHUNKS, range(CHUNKS - CROSS), 3)
        arrive(CHUNKS + 2, crossing, 3)
    due.sort(key=lambda event: event[0])
    return own, [event[1:] for event in due]


def dot_t(a, b):
    return lax.dot_general(a, b, (((1,), (1,)), ((), ())), preferred_element_type=jnp.float32)


def kernel(n, roots, off, listed, res, sub, inv, work, sub_v, coef, table, res_v, gram_sum, gram_hi, gram_lo, corr,
           partial, inbox, slabs, strips, diag_out, diag_in, diag, tree_out, tree_in,
           load_sem, hop_send, hop_recv, swap_send, swap_recv, rs_send, rs_recv, ag_send, ag_recv,
           tree_send, tree_recv, diag_send, diag_recv, pair_send, pair_recv):
    me = lax.axis_index("tr")
    root = lax.axis_index("root")
    rows, cols = res.shape
    blk = inv.shape[1]
    spans = sub.shape[0]
    blocks = cols // blk
    share = blk // roots
    owners = slabs.shape[1]
    base = (n - owners) // 2
    width = spans // owners
    chunk = share // CHUNKS
    shared = strips is not None
    half = spans // roots

    def block(b):
        return pl.ds(b * blk, blk)

    own_load = pltpu.make_async_copy(inv.at[0], table.at[0], load_sem.at[0])
    res_load = pltpu.make_async_copy(res, res_v, load_sem.at[1])
    sub_load = pltpu.make_async_copy(sub, sub_v, load_sem.at[2])
    sub_load.start()
    own_load.start()
    res_load.start()

    def is_owner(device):
        return jnp.logical_and(device >= base, device < base + owners)

    side = lax.rem(me, 2)
    twin = me + 1 - 2 * side
    peers = {"twin": twin, "near": lax.rem(me + n - 2, n), "cross": lax.rem(me + n - 1, n)}

    barrier = pltpu.get_barrier_semaphore()

    def linked(d):
        peer = lax.rem(me + d + 1, n)
        close = jnp.logical_or(jnp.logical_or(d + 1 == 2, d + 1 == n - 2), peer == twin)
        return jnp.logical_or(close, jnp.logical_or(is_owner(me), is_owner(peer)))

    def greet(d):
        def signal():
            pl.semaphore_signal(barrier, inc=1, device_id={"tr": lax.rem(me + d + 1, n)}, device_id_type=MESH)

        pl.when(linked(d))(signal)

    for d in range(1, roots):
        pl.semaphore_signal(barrier, inc=1, device_id={"root": lax.rem(root + d, roots)}, device_id_type=MESH)
    each(n - 1, greet)
    partners = lax.fori_loop(0, n - 1, lambda d, c: c + linked(d).astype(jnp.int32), jnp.int32(roots - 1))
    pl.semaphore_wait(barrier, partners)

    def chunk_rows(half, q):
        return pl.ds(pl.multiple_of(half * share + q * chunk, chunk), chunk)

    def hop(src, q, slot, peer, sem):
        return pltpu.make_async_remote_copy(
            src_ref=src, dst_ref=table.at[slot, chunk_rows(root, q)],
            send_sem=hop_send.at[sem, q], recv_sem=hop_recv.at[slot, q],
            device_id={"tr": peers[peer]}, device_id_type=MESH)

    def own_hop(q, slot, peer, sem):
        return hop(inv.at[0, chunk_rows(root, q)], q, slot, peer, sem)

    def relay(e, q, slot, peer, sem):
        return hop(table.at[e, chunk_rows(root, q)], q, slot, peer, sem)

    def swap(e, q, half):
        rows_q = table.at[e, chunk_rows(half, q)]
        return pltpu.make_async_remote_copy(
            src_ref=rows_q, dst_ref=rows_q,
            send_sem=swap_send.at[e, q], recv_sem=swap_recv.at[e, q],
            device_id={"root": 1 - root}, device_id_type=MESH)

    def gram_step(b):
        mine = sub_v[pl.ds(pl.multiple_of(root * half, half), half), block(b)] if shared else sub_v[:, block(b)]
        part = dot_t(sub_v[:, block(b)], mine)
        gram_sum[...] = part if b == 0 else gram_sum[...] + part

    lower = me < n // 2
    toward = jnp.where(lower, me + 2, me - 2)
    beyond = jnp.where(lower, me + 4, me - 4)

    def strip(k, beside=False):
        owner = (1 - side if beside else side) + 2 * k
        return pl.ds(pl.multiple_of(owner * width, width), width)

    def tree_copy(k, peer):
        return pltpu.make_async_remote_copy(
            src_ref=tree_out.at[k], dst_ref=tree_in.at[k], send_sem=tree_send.at[k], recv_sem=tree_recv.at[k],
            device_id={"tr": peer}, device_id_type=MESH)

    def diag_copy(t):
        return pltpu.make_async_remote_copy(
            src_ref=diag_out.at[t], dst_ref=diag_in.at[me], send_sem=diag_send.at[t], recv_sem=diag_recv.at[me],
            device_id={"tr": base + 2 * root + t}, device_id_type=MESH)

    def diag_from(peer):
        return pltpu.make_async_remote_copy(
            src_ref=diag_out.at[0], dst_ref=diag_in.at[peer], send_sem=diag_send.at[0], recv_sem=diag_recv.at[peer],
            device_id={"tr": peer}, device_id_type=MESH)

    def pair_copy(ref, k):
        return pltpu.make_async_remote_copy(
            src_ref=ref, dst_ref=ref, send_sem=pair_send.at[k], recv_sem=pair_recv.at[k],
            device_id={"root": 1 - root}, device_id_type=MESH)

    def for_own_diag(body):
        for t in range(2):
            pl.when(me != base + 2 * root + t)(functools.partial(body, t))

    def start_tree():
        shape = (width, width)
        on = lax.broadcasted_iota(jnp.int32, shape, 0) == lax.broadcasted_iota(jnp.int32, shape, 1)
        for t in range(2):
            place = pl.ds(pl.multiple_of((2 * root + t) * width, width), width)
            span = pl.ds(t * width, width)
            square = gram_sum[place, span]
            line = jnp.sum(jnp.where(on, square, 0.0), axis=0, keepdims=True)
            diag_out[t] = jnp.broadcast_to(line, diag_out.shape[1:])
            gram_sum[place, span] = jnp.where(on, 0.0, square)
        for k in range(2):
            tree_out[k] = gram_sum[strip(k, beside=True), :].astype(LINK)
            tree_copy(k, twin).start()
        for_own_diag(lambda t: diag_copy(t).start())

    def half_rows(far):
        k = lower.astype(jnp.int32) if far else 1 - lower.astype(jnp.int32)
        return pl.ds(pl.multiple_of((side + 2 * k) * width, width), width)

    def sum_twins():
        for k in range(2):
            tree_copy(k, twin).wait_recv()
            gram_sum[strip(k), :] += tree_in[k].astype(jnp.float32)

        def outer():
            tree_out[3] = gram_sum[half_rows(True), :].astype(LINK)
            tree_copy(3, beyond).start()
            tree_out[2] = gram_sum[half_rows(False), :].astype(LINK)
            tree_copy(2, toward).start()

        def inner():
            tree_out[4] = gram_sum[half_rows(True), :].astype(LINK)
            tree_copy(4, toward).start()

        pl.when(jnp.logical_not(is_owner(me)))(outer)
        pl.when(is_owner(me))(inner)

    def sum_inner():
        total = gram_sum[half_rows(False), :]
        for k in (4, 2, 3):
            tree_copy(k, toward).wait_recv()
            total += tree_in[k].astype(jnp.float32)
        strips[root] = total.astype(LINK)
        pair_copy(strips.at[root], 0).start()

        def sum_diag():
            diag_in[me] = diag_out[lax.rem(me - base, 2)]
            each(n - 1, lambda d: diag_from(lax.rem(me + d + 1, n)).wait_recv())
            diag[...] = jnp.sum(diag_in[...], axis=0)
            pair_copy(diag, 1).start()

        pl.when((me - base) // 2 == root)(sum_diag)

    def paired():
        pair_copy(strips.at[1 - root], 0).wait_recv()
        pl.when((me - base) // 2 != root)(lambda: pair_copy(diag, 1).wait_recv())

    def exchange(s):
        own, order = flows(s)
        for j, (chunks, slot, peer) in enumerate(own):
            for q in chunks:
                own_hop(q, slot, peer, j).start()
        sub_load.wait()
        for i, (e, q, targets) in enumerate(order):
            if i < blocks:
                gram_step(i)
            if shared and i == TREE_AT:
                start_tree()
            relay(e, q, e, "twin", 0).wait_recv()
            for j, (slot, peer) in enumerate(targets):
                relay(e, q, slot, peer, 2 + e if j == 0 else 2 + OFFS).start()
            swap(e, q, root).start()

    def close(s):
        own, order = flows(s)
        for j, (chunks, slot, peer) in enumerate(own):
            for q in chunks:
                own_hop(q, slot, peer, j).wait_send()
        for e, q, targets in order:
            for j, (slot, peer) in enumerate(targets):
                relay(e, q, slot, peer, 2 + e if j == 0 else 2 + OFFS).wait_send()
            swap(e, q, root).wait_send()

    for s in range(2):
        pl.when(side == s)(functools.partial(exchange, s))
    if not shared:
        high = gram_sum[...].astype(jnp.bfloat16)
        gram_hi[...] = high
        gram_lo[...] = (gram_sum[...] - high.astype(jnp.float32)).astype(jnp.bfloat16)
    own_load.wait()
    res_load.wait()
    for e in range(1, OFFS):
        for q in range(CHUNKS):
            swap(e, q, 1 - root).wait_recv()

    def rs_copy(i, j):
        return pltpu.make_async_remote_copy(
            src_ref=partial.at[i, j], dst_ref=inbox.at[i, me],
            send_sem=rs_send.at[i, j], recv_sem=rs_recv.at[i, me],
            device_id={"tr": base + j}, device_id_type=MESH)

    def rs_in(i, peer):
        return pltpu.make_async_remote_copy(
            src_ref=inbox.at[i, peer], dst_ref=inbox.at[i, peer],
            send_sem=rs_send.at[i, 0], recv_sem=rs_recv.at[i, peer],
            device_id={"tr": peer}, device_id_type=MESH)

    def ag_copy(i, peer):
        return pltpu.make_async_remote_copy(
            src_ref=slabs.at[i, me - base], dst_ref=slabs.at[i, me - base],
            send_sem=ag_send.at[i, peer], recv_sem=ag_recv.at[i, me - base],
            device_id={"tr": peer}, device_id_type=MESH)

    def ag_in(i, j):
        return pltpu.make_async_remote_copy(
            src_ref=slabs.at[i, j], dst_ref=slabs.at[i, j],
            send_sem=ag_send.at[i, 0], recv_sem=ag_recv.at[i, j],
            device_id={"tr": base + j}, device_id_type=MESH)

    def rest(d):
        return lax.rem(base + owners + d, n)

    def for_other_owners(body):
        for j in range(owners):
            pl.when(me != base + j)(functools.partial(body, j))

    def send_slab(i, value):
        slabs[i, me - base] = value
        for_other_owners(lambda j: ag_copy(i, base + j).start())
        each(n - owners, lambda d: ag_copy(i, rest(d)).start())

    def own_sum(i):
        inbox[i, me] = partial[i, me - base]
        each(n - 1, lambda d: rs_in(i, lax.rem(me + d + 1, n)).wait_recv())
        total = jnp.sum(inbox[i].astype(jnp.float32), axis=0)
        send_slab(i, total.astype(jnp.bfloat16))
        if shared:
            sum_inner()
            for k in range(2):
                arrive(i, k)
            first = all_gathered(i)
            paired()
            again = sum(
                dot_t(first[:, h * half:(h + 1) * half], strips[h]) for h in range(roots))
            own = slabs[i, me - base].astype(jnp.float32)
            send_slab(i + 1, (total - (again + own * diag[pl.ds(0, 1), :])).astype(jnp.bfloat16))

    group = owners // 2
    reach = group * width
    near_group = jnp.where(me < n // 2, 0, 1)
    far_group = 1 - near_group

    def reach_of(k):
        return pl.ds(k * reach, reach) if isinstance(k, int) else pl.ds(pl.multiple_of(k * reach, reach), reach)

    def scatter(i, k, total):
        for t in range(group):
            j = k * group + t
            partial[i, j] = total[:, t * width:(t + 1) * width].astype(partial.dtype)
            pl.when(me != base + j)(rs_copy(i, j).start)

    def arrive(i, k):
        for t in range(group):
            j = k * group + t
            pl.when(me != base + j)(ag_in(i, j).wait_recv)

    def gathered(i, k):
        return jnp.concatenate([slabs[i, k * group + t] for t in range(group)], axis=1)

    def all_gathered(i):
        return jnp.concatenate([gathered(i, k) for k in range(2)], axis=1)

    def update(first):
        for b in range(blocks):
            work[:, block(b)] -= jnp.dot(first, sub_v[:, block(b)], preferred_element_type=jnp.float32)

    for stage, k in enumerate((far_group, near_group)):
        total = jnp.zeros((rows, reach), jnp.float32)
        for b in range(blocks):
            if stage == 0:
                x = res_v[:, block(b)]
                solved = jnp.dot(x, table[off[b]], preferred_element_type=jnp.float32)
                kept = jnp.where(listed[b] > 0, solved, x.astype(jnp.float32))
                work[:, block(b)] = kept
                rounded = kept.astype(jnp.bfloat16)
                res_v[:, block(b)] = rounded
            else:
                rounded = res_v[:, block(b)]
            total += dot_t(rounded, sub_v[reach_of(k), block(b)])
        if not shared:
            corr[:, reach_of(k)] = total
        scatter(0, k, total)
    if shared:
        sum_twins()
    pl.when(is_owner(me))(functools.partial(own_sum, 0))

    def arrive_all(i):
        for k in range(2):
            arrive(i, k)

    if shared:
        pl.when(jnp.logical_not(is_owner(me)))(functools.partial(arrive_all, 0))
    else:
        arrive_all(0)
    first = all_gathered(0)
    if not shared:
        total = corr[...] - (
            jnp.dot(first, gram_hi[...], preferred_element_type=jnp.float32)
            + jnp.dot(first, gram_lo[...], preferred_element_type=jnp.float32))
        for k in range(2):
            scatter(1, k, total[:, k * reach:(k + 1) * reach])
        pl.when(is_owner(me))(functools.partial(own_sum, 1))
    update(first)
    for s in range(2):
        pl.when(side == s)(functools.partial(close, s))
    arrive(1, near_group)
    near = gathered(1, near_group)
    for b in range(blocks):
        work[:, block(b)] -= jnp.dot(near, sub_v[reach_of(near_group), block(b)], preferred_element_type=jnp.float32)
    arrive(1, far_group)
    coef[...] = gathered(1, far_group)

    for i in range(PASSES):
        if not (shared and i):
            for_other_owners(lambda j: rs_copy(i, j).wait_send())

        def sent():
            for_other_owners(lambda j: ag_copy(i, base + j).wait_send())
            each(n - owners, lambda d: ag_copy(i, rest(d)).wait_send())

        pl.when(is_owner(me))(sent)
    if shared:
        for k in range(2):
            tree_copy(k, twin).wait_send()
        for_own_diag(lambda t: diag_copy(t).wait_send())

        def inner_sent():
            tree_copy(4, toward).wait_send()
            pair_copy(strips.at[root], 0).wait_send()
            pl.when((me - base) // 2 == root)(lambda: pair_copy(diag, 1).wait_send())

        def outer_sent():
            tree_copy(2, toward).wait_send()
            tree_copy(3, beyond).wait_send()

        pl.when(is_owner(me))(inner_sent)
        pl.when(jnp.logical_not(is_owner(me)))(outer_sent)


def finish(n, blk, work, sub_v, coef, out, out_v, out_sem):
    blocks = work.shape[1] // blk
    reach = coef.shape[1]
    far = pl.ds(pl.multiple_of(jnp.where(lax.axis_index("tr") < n // 2, 1, 0) * reach, reach), reach)

    def store(b):
        cols = pl.ds(b * blk, blk)
        return pltpu.make_async_copy(out_v.at[:, cols], out.at[:, cols], out_sem.at[b])

    for b in range(blocks):
        cols = pl.ds(b * blk, blk)
        out_v[:, cols] = work[:, cols] - jnp.dot(coef[...], sub_v[far, cols], preferred_element_type=jnp.float32)
        store(b).start()
    for b in range(blocks):
        store(b).wait()


def per_device(n, roots, residual, subspace, inverses, owner_offset, listed):
    rows, cols = residual.shape
    spans = subspace.shape[0]
    blk = inverses.shape[1]
    blocks = cols // blk
    owners = min(n // 2, spans // LANES)
    width = spans // owners
    hbm = pl.BlockSpec(memory_space=pl.ANY)
    smem = pl.BlockSpec(memory_space=pltpu.SMEM)
    vmem = pl.BlockSpec(memory_space=pltpu.VMEM)
    dma = pltpu.SemaphoreType.DMA
    shared = roots == 2 and owners == 4 and n == 2 * owners
    f32, bf16 = jnp.float32, jnp.bfloat16
    if shared:
        gram = {
            "gram_sum": pltpu.VMEM((spans, spans // roots), f32),
            "strips": pltpu.VMEM((roots, width, spans // roots), LINK),
            "diag_out": pltpu.VMEM((2, SUBLANES, width), f32), "diag_in": pltpu.VMEM((n, SUBLANES, width), f32),
            "diag": pltpu.VMEM((SUBLANES, width), f32),
            "tree_out": pltpu.VMEM((5, width, spans // roots), LINK),
            "tree_in": pltpu.VMEM((5, width, spans // roots), LINK),
            "tree_send": dma((5,)), "tree_recv": dma((5,)), "diag_send": dma((2,)), "diag_recv": dma((n,)),
            "pair_send": dma((2,)), "pair_recv": dma((2,)),
        }
        rounds = 1
    else:
        gram = {
            "gram_sum": pltpu.VMEM((spans, spans), f32), "corr": pltpu.VMEM((rows, spans), f32),
            "gram_hi": pltpu.VMEM((spans, spans), bf16), "gram_lo": pltpu.VMEM((spans, spans), bf16),
        }
        rounds = PASSES
    scratch = {
        "table": pltpu.VMEM((OFFS, blk, blk), bf16), "res_v": pltpu.VMEM((rows, cols), bf16),
        "partial": pltpu.VMEM((rounds, owners, rows, width), LINK),
        "inbox": pltpu.VMEM((rounds, n, rows, width), LINK),
        "slabs": pltpu.VMEM((PASSES, owners, rows, width), bf16),
        "load_sem": dma((3,)),
        "hop_send": dma((OFFS + 3, CHUNKS)), "hop_recv": dma((OFFS, CHUNKS)),
        "swap_send": dma((OFFS, CHUNKS)), "swap_recv": dma((OFFS, CHUNKS)),
        "rs_send": dma((rounds, owners)), "rs_recv": dma((rounds, n)),
        "ag_send": dma((PASSES, n)), "ag_recv": dma((PASSES, owners)),
        **gram,
    }
    absent = dict.fromkeys(
        ("gram_hi", "gram_lo", "corr", "strips", "diag_out", "diag_in", "diag", "tree_out", "tree_in",
         "tree_send", "tree_recv", "diag_send", "diag_recv", "pair_send", "pair_recv"))

    def body(off, listed, res, sub, inv, work, sub_v, coef, *refs):
        kernel(n, roots, off, listed, res, sub, inv, work, sub_v, coef, **{**absent, **dict(zip(scratch, refs))})

    held = pl.pallas_call(
        body,
        out_shape=(
            pltpu.VMEM((rows, cols), jnp.float32),
            pltpu.VMEM((spans, cols), jnp.bfloat16),
            pltpu.VMEM((rows, spans // 2), jnp.bfloat16),
        ),
        in_specs=[smem, smem, hbm, hbm, hbm],
        out_specs=(vmem, vmem, vmem),
        scratch_shapes=list(scratch.values()),
        compiler_params=pltpu.CompilerParams(
            collective_id=0, has_side_effects=True, vmem_limit_bytes=VMEM_GRANT),
    )(owner_offset, listed, residual, subspace, inverses)
    return pl.pallas_call(
        functools.partial(finish, n, blk),
        out_shape=jax.ShapeDtypeStruct((rows, cols), jnp.float32),
        in_specs=[vmem, vmem, vmem],
        out_specs=hbm,
        scratch_shapes=[pltpu.VMEM((rows, cols), jnp.float32), dma((blocks,))],
        compiler_params=pltpu.CompilerParams(vmem_limit_bytes=16 * 2**20),
    )(*held)


def solution(mesh):
    body = functools.partial(per_device, mesh.shape["tr"], mesh.shape["root"])
    return jax.shard_map(
        body,
        mesh=mesh,
        in_specs=(
            P("root", ("grp", "tr")),
            P(None, ("grp", "tr")),
            P(("grp", "tr"), None, None),
            P(("grp", "tr")),
            P(("grp", "tr")),
        ),
        out_specs=P("root", ("grp", "tr")),
        check_vma=False,
    )
```

```python
import functools
import jax
import jax.numpy as jnp
from jax import lax
from jax.experimental import pallas as pl
from jax.experimental.pallas import tpu as pltpu
from jax.sharding import PartitionSpec as P

OFFS = 4
PASSES = 2
LINK = jnp.bfloat16
SUBLANES = 8
LANES = 128
CHUNKS = 8
LOW = 0
BOTH = 4
CROSS = 3
LEAD = 3.5
TREE_AT = 23
MESH = pl.DeviceIdType.MESH
VMEM_GRANT = 61_700_000


def each(count, body):
    if count <= 16:
        for i in range(count):
            body(i)
    else:
        pl.loop(0, count)(body)


def flows(side):
    every, low, both, high = range(CHUNKS), range(LOW), range(LOW, LOW + BOTH), range(LOW + BOTH, CHUNKS)
    crossing = range(CHUNKS - CROSS, CHUNKS)
    due = []

    def arrive(start, chunks, slot, *targets):
        for i, q in enumerate(chunks):
            due.append((start + i, slot, q, [(there, peer) for there, peer, among in targets if q in among]))

    if side == 0:
        own = [(every, 2, "near")]
        arrive(0, every, 2, (1, "twin", every), (3, "cross", crossing))
        arrive(0.5, every, 1, (3, "near", range(LOW + BOTH)))
        arrive(CHUNKS, low, 3, (2, "twin", every))
        arrive(CHUNKS, both, 3)
        arrive(CHUNKS, high, 3)
    else:
        own = [(every, 1, "twin"), (both, 2, "near"), (high, 2, "near")]
        arrive(len(both), high, 2, (3, "twin", every))
        arrive(0, both, 2)
        arrive(LEAD, every, 1, (3, "near", range(CHUNKS - CROSS)))
        arrive(CHUNKS + LEAD, low, 2)
        arrive(CHUNKS, range(CHUNKS - CROSS), 3)
        arrive(CHUNKS + 2, crossing, 3)
    due.sort(key=lambda event: event[0])
    return own, [event[1:] for event in due]


def dot_t(a, b):
    return lax.dot_general(a, b, (((1,), (1,)), ((), ())), preferred_element_type=jnp.float32)


def kernel(n, roots, off, listed, res, sub, inv, work, sub_v, coef, table, res_v, gram_sum, gram_hi, gram_lo, corr,
           partial, inbox, slabs, strips, diag_out, diag_in, diag, tree_out, tree_in,
           load_sem, hop_send, hop_recv, swap_send, swap_recv, rs_send, rs_recv, ag_send, ag_recv,
           tree_send, tree_recv, diag_send, diag_recv, pair_send, pair_recv):
    me = lax.axis_index("tr")
    root = lax.axis_index("root")
    rows, cols = res.shape
    blk = inv.shape[1]
    spans = sub.shape[0]
    blocks = cols // blk
    share = blk // roots
    owners = slabs.shape[1]
    base = (n - owners) // 2
    width = spans // owners
    chunk = share // CHUNKS
    shared = strips is not None
    half = spans // roots

    def block(b):
        return pl.ds(b * blk, blk)

    own_load = pltpu.make_async_copy(inv.at[0], table.at[0], load_sem.at[0])
    res_load = pltpu.make_async_copy(res, res_v, load_sem.at[1])
    sub_load = pltpu.make_async_copy(sub, sub_v, load_sem.at[2])
    sub_load.start()
    own_load.start()
    res_load.start()

    def is_owner(device):
        return jnp.logical_and(device >= base, device < base + owners)

    side = lax.rem(me, 2)
    twin = me + 1 - 2 * side
    peers = {"twin": twin, "near": lax.rem(me + n - 2, n), "cross": lax.rem(me + n - 1, n)}

    barrier = pltpu.get_barrier_semaphore()

    def linked(d):
        peer = lax.rem(me + d + 1, n)
        close = jnp.logical_or(jnp.logical_or(d + 1 == 2, d + 1 == n - 2), peer == twin)
        return jnp.logical_or(close, jnp.logical_or(is_owner(me), is_owner(peer)))

    def greet(d):
        def signal():
            pl.semaphore_signal(barrier, inc=1, device_id={"tr": lax.rem(me + d + 1, n)}, device_id_type=MESH)

        pl.when(linked(d))(signal)

    for d in range(1, roots):
        pl.semaphore_signal(barrier, inc=1, device_id={"root": lax.rem(root + d, roots)}, device_id_type=MESH)
    each(n - 1, greet)
    partners = lax.fori_loop(0, n - 1, lambda d, c: c + linked(d).astype(jnp.int32), jnp.int32(roots - 1))
    pl.semaphore_wait(barrier, partners)

    def chunk_rows(half, q):
        return pl.ds(pl.multiple_of(half * share + q * chunk, chunk), chunk)

    def hop(src, q, slot, peer, sem):
        return pltpu.make_async_remote_copy(
            src_ref=src, dst_ref=table.at[slot, chunk_rows(root, q)],
            send_sem=hop_send.at[sem, q], recv_sem=hop_recv.at[slot, q],
            device_id={"tr": peers[peer]}, device_id_type=MESH)

    def own_hop(q, slot, peer, sem):
        return hop(inv.at[0, chunk_rows(root, q)], q, slot, peer, sem)

    def relay(e, q, slot, peer, sem):
        return hop(table.at[e, chunk_rows(root, q)], q, slot, peer, sem)

    def swap(e, q, half):
        rows_q = table.at[e, chunk_rows(half, q)]
        return pltpu.make_async_remote_copy(
            src_ref=rows_q, dst_ref=rows_q,
            send_sem=swap_send.at[e, q], recv_sem=swap_recv.at[e, q],
            device_id={"root": 1 - root}, device_id_type=MESH)

    def gram_step(b):
        mine = sub_v[pl.ds(pl.multiple_of(root * half, half), half), block(b)] if shared else sub_v[:, block(b)]
        part = dot_t(sub_v[:, block(b)], mine)
        gram_sum[...] = part if b == 0 else gram_sum[...] + part

    lower = me < n // 2
    toward = jnp.where(lower, me + 2, me - 2)
    beyond = jnp.where(lower, me + 4, me - 4)

    def strip(k, beside=False):
        owner = (1 - side if beside else side) + 2 * k
        return pl.ds(pl.multiple_of(owner * width, width), width)

    def tree_copy(k, peer):
        return pltpu.make_async_remote_copy(
            src_ref=tree_out.at[k], dst_ref=tree_in.at[k], send_sem=tree_send.at[k], recv_sem=tree_recv.at[k],
            device_id={"tr": peer}, device_id_type=MESH)

    def diag_copy(t):
        return pltpu.make_async_remote_copy(
            src_ref=diag_out.at[t], dst_ref=diag_in.at[me], send_sem=diag_send.at[t], recv_sem=diag_recv.at[me],
            device_id={"tr": base + 2 * root + t}, device_id_type=MESH)

    def diag_from(peer):
        return pltpu.make_async_remote_copy(
            src_ref=diag_out.at[0], dst_ref=diag_in.at[peer], send_sem=diag_send.at[0], recv_sem=diag_recv.at[peer],
            device_id={"tr": peer}, device_id_type=MESH)

    def pair_copy(ref, k):
        return pltpu.make_async_remote_copy(
            src_ref=ref, dst_ref=ref, send_sem=pair_send.at[k], recv_sem=pair_recv.at[k],
            device_id={"root": 1 - root}, device_id_type=MESH)

    def for_own_diag(body):
        for t in range(2):
            pl.when(me != base + 2 * root + t)(functools.partial(body, t))

    def start_tree():
        shape = (width, width)
        on = lax.broadcasted_iota(jnp.int32, shape, 0) == lax.broadcasted_iota(jnp.int32, shape, 1)
        for t in range(2):
            place = pl.ds(pl.multiple_of((2 * root + t) * width, width), width)
            span = pl.ds(t * width, width)
            square = gram_sum[place, span]
            line = jnp.sum(jnp.where(on, square, 0.0), axis=0, keepdims=True)
            diag_out[t] = jnp.broadcast_to(line, diag_out.shape[1:])
            gram_sum[place, span] = jnp.where(on, 0.0, square)
        for k in range(2):
            tree_out[k] = gram_sum[strip(k, beside=True), :].astype(LINK)
            tree_copy(k, twin).start()
        for_own_diag(lambda t: diag_copy(t).start())

    def half_rows(far):
        k = lower.astype(jnp.int32) if far else 1 - lower.astype(jnp.int32)
        return pl.ds(pl.multiple_of((side + 2 * k) * width, width), width)

    def sum_twins():
        for k in range(2):
            tree_copy(k, twin).wait_recv()
            gram_sum[strip(k), :] += tree_in[k].astype(jnp.float32)

        def outer():
            tree_out[3] = gram_sum[half_rows(True), :].astype(LINK)
            tree_copy(3, beyond).start()
            tree_out[2] = gram_sum[half_rows(False), :].astype(LINK)
            tree_copy(2, toward).start()

        def inner():
            tree_out[4] = gram_sum[half_rows(True), :].astype(LINK)
            tree_copy(4, toward).start()

        pl.when(jnp.logical_not(is_owner(me)))(outer)
        pl.when(is_owner(me))(inner)

    def sum_inner():
        total = gram_sum[half_rows(False), :]
        for k in (4, 2, 3):
            tree_copy(k, toward).wait_recv()
            total += tree_in[k].astype(jnp.float32)
        strips[root] = total.astype(LINK)
        pair_copy(strips.at[root], 0).start()

        def sum_diag():
            diag_in[me] = diag_out[lax.rem(me - base, 2)]
            each(n - 1, lambda d: diag_from(lax.rem(me + d + 1, n)).wait_recv())
            diag[...] = jnp.sum(diag_in[...], axis=0)
            pair_copy(diag, 1).start()

        pl.when((me - base) // 2 == root)(sum_diag)

    def paired():
        pair_copy(strips.at[1 - root], 0).wait_recv()
        pl.when((me - base) // 2 != root)(lambda: pair_copy(diag, 1).wait_recv())

    def exchange(s):
        own, order = flows(s)
        for j, (chunks, slot, peer) in enumerate(own):
            for q in chunks:
                own_hop(q, slot, peer, j).start()
        sub_load.wait()
        for i, (e, q, targets) in enumerate(order):
            if i < blocks:
                gram_step(i)
            if shared and i == TREE_AT:
                start_tree()
            relay(e, q, e, "twin", 0).wait_recv()
            for j, (slot, peer) in enumerate(targets):
                relay(e, q, slot, peer, 2 + e if j == 0 else 2 + OFFS).start()
            swap(e, q, root).start()

    def close(s):
        own, order = flows(s)
        for j, (chunks, slot, peer) in enumerate(own):
            for q in chunks:
                own_hop(q, slot, peer, j).wait_send()
        for e, q, targets in order:
            for j, (slot, peer) in enumerate(targets):
                relay(e, q, slot, peer, 2 + e if j == 0 else 2 + OFFS).wait_send()
            swap(e, q, root).wait_send()

    for s in range(2):
        pl.when(side == s)(functools.partial(exchange, s))
    if not shared:
        high = gram_sum[...].astype(jnp.bfloat16)
        gram_hi[...] = high
        gram_lo[...] = (gram_sum[...] - high.astype(jnp.float32)).astype(jnp.bfloat16)
    own_load.wait()
    res_load.wait()
    for e in range(1, OFFS):
        for q in range(CHUNKS):
            swap(e, q, 1 - root).wait_recv()

    def rs_copy(i, j):
        return pltpu.make_async_remote_copy(
            src_ref=partial.at[i, j], dst_ref=inbox.at[i, me],
            send_sem=rs_send.at[i, j], recv_sem=rs_recv.at[i, me],
            device_id={"tr": base + j}, device_id_type=MESH)

    def rs_in(i, peer):
        return pltpu.make_async_remote_copy(
            src_ref=inbox.at[i, peer], dst_ref=inbox.at[i, peer],
            send_sem=rs_send.at[i, 0], recv_sem=rs_recv.at[i, peer],
            device_id={"tr": peer}, device_id_type=MESH)

    def ag_copy(i, peer):
        return pltpu.make_async_remote_copy(
            src_ref=slabs.at[i, me - base], dst_ref=slabs.at[i, me - base],
            send_sem=ag_send.at[i, peer], recv_sem=ag_recv.at[i, me - base],
            device_id={"tr": peer}, device_id_type=MESH)

    def ag_in(i, j):
        return pltpu.make_async_remote_copy(
            src_ref=slabs.at[i, j], dst_ref=slabs.at[i, j],
            send_sem=ag_send.at[i, 0], recv_sem=ag_recv.at[i, j],
            device_id={"tr": base + j}, device_id_type=MESH)

    def rest(d):
        return lax.rem(base + owners + d, n)

    def for_other_owners(body):
        for j in range(owners):
            pl.when(me != base + j)(functools.partial(body, j))

    def send_slab(i, value):
        slabs[i, me - base] = value
        for_other_owners(lambda j: ag_copy(i, base + j).start())
        each(n - owners, lambda d: ag_copy(i, rest(d)).start())

    def own_sum(i):
        inbox[i, me] = partial[i, me - base]
        each(n - 1, lambda d: rs_in(i, lax.rem(me + d + 1, n)).wait_recv())
        total = jnp.sum(inbox[i].astype(jnp.float32), axis=0)
        send_slab(i, total.astype(jnp.bfloat16))
        if shared:
            sum_inner()
            for k in range(2):
                arrive(i, k)
            first = all_gathered(i)
            paired()
            again = sum(
                dot_t(first[:, h * half:(h + 1) * half], strips[h]) for h in range(roots))
            own = slabs[i, me - base].astype(jnp.float32)
            send_slab(i + 1, (total - (again + own * diag[pl.ds(0, 1), :])).astype(jnp.bfloat16))

    group = owners // 2
    reach = group * width
    near_group = jnp.where(me < n // 2, 0, 1)
    far_group = 1 - near_group

    def reach_of(k):
        return pl.ds(k * reach, reach) if isinstance(k, int) else pl.ds(pl.multiple_of(k * reach, reach), reach)

    def scatter(i, k, total):
        for t in range(group):
            j = k * group + t
            partial[i, j] = total[:, t * width:(t + 1) * width].astype(partial.dtype)
            pl.when(me != base + j)(rs_copy(i, j).start)

    def arrive(i, k):
        for t in range(group):
            j = k * group + t
            pl.when(me != base + j)(ag_in(i, j).wait_recv)

    def gathered(i, k):
        return jnp.concatenate([slabs[i, k * group + t] for t in range(group)], axis=1)

    def all_gathered(i):
        return jnp.concatenate([gathered(i, k) for k in range(2)], axis=1)

    def update(first):
        for b in range(blocks):
            work[:, block(b)] -= jnp.dot(first, sub_v[:, block(b)], preferred_element_type=jnp.float32)

    for stage, k in enumerate((far_group, near_group)):
        total = jnp.zeros((rows, reach), jnp.float32)
        for b in range(blocks):
            if stage == 0:
                x = res_v[:, block(b)]
                solved = jnp.dot(x, table[off[b]], preferred_element_type=jnp.float32)
                kept = jnp.where(listed[b] > 0, solved, x.astype(jnp.float32))
                work[:, block(b)] = kept
                rounded = kept.astype(jnp.bfloat16)
                res_v[:, block(b)] = rounded
            else:
                rounded = res_v[:, block(b)]
            total += dot_t(rounded, sub_v[reach_of(k), block(b)])
        if not shared:
            corr[:, reach_of(k)] = total
        scatter(0, k, total)
    if shared:
        sum_twins()
    pl.when(is_owner(me))(functools.partial(own_sum, 0))

    def arrive_all(i):
        for k in range(2):
            arrive(i, k)

    if shared:
        pl.when(jnp.logical_not(is_owner(me)))(functools.partial(arrive_all, 0))
    else:
        arrive_all(0)
    first = all_gathered(0)
    if not shared:
        total = corr[...] - (
            jnp.dot(first, gram_hi[...], preferred_element_type=jnp.float32)
            + jnp.dot(first, gram_lo[...], preferred_element_type=jnp.float32))
        for k in range(2):
            scatter(1, k, total[:, k * reach:(k + 1) * reach])
        pl.when(is_owner(me))(functools.partial(own_sum, 1))
    update(first)
    for s in range(2):
        pl.when(side == s)(functools.partial(close, s))
    arrive(1, near_group)
    near = gathered(1, near_group)
    for b in range(blocks):
        work[:, block(b)] -= jnp.dot(near, sub_v[reach_of(near_group), block(b)], preferred_element_type=jnp.float32)
    for i in range(PASSES):
        if not (shared and i):
            for_other_owners(lambda j: rs_copy(i, j).wait_send())

        def sent():
            for_other_owners(lambda j: ag_copy(i, base + j).wait_send())
            each(n - owners, lambda d: ag_copy(i, rest(d)).wait_send())

        pl.when(is_owner(me))(sent)
    if shared:
        for k in range(2):
            tree_copy(k, twin).wait_send()
        for_own_diag(lambda t: diag_copy(t).wait_send())

        def inner_sent():
            tree_copy(4, toward).wait_send()
            pair_copy(strips.at[root], 0).wait_send()
            pl.when((me - base) // 2 == root)(lambda: pair_copy(diag, 1).wait_send())

        def outer_sent():
            tree_copy(2, toward).wait_send()
            tree_copy(3, beyond).wait_send()

        pl.when(is_owner(me))(inner_sent)
        pl.when(jnp.logical_not(is_owner(me)))(outer_sent)

    arrive(1, far_group)
    coef[...] = gathered(1, far_group)


def finish(n, blk, work, sub_v, coef, out, out_v, out_sem):
    blocks = work.shape[1] // blk
    reach = coef.shape[1]
    far = pl.ds(pl.multiple_of(jnp.where(lax.axis_index("tr") < n // 2, 1, 0) * reach, reach), reach)

    def store(b):
        cols = pl.ds(b * blk, blk)
        return pltpu.make_async_copy(out_v.at[:, cols], out.at[:, cols], out_sem.at[b])

    for b in range(blocks):
        cols = pl.ds(b * blk, blk)
        out_v[:, cols] = work[:, cols] - jnp.dot(coef[...], sub_v[far, cols], preferred_element_type=jnp.float32)
        store(b).start()
    for b in range(blocks):
        store(b).wait()


def per_device(n, roots, residual, subspace, inverses, owner_offset, listed):
    rows, cols = residual.shape
    spans = subspace.shape[0]
    blk = inverses.shape[1]
    blocks = cols // blk
    owners = min(n // 2, spans // LANES)
    width = spans // owners
    hbm = pl.BlockSpec(memory_space=pl.ANY)
    smem = pl.BlockSpec(memory_space=pltpu.SMEM)
    vmem = pl.BlockSpec(memory_space=pltpu.VMEM)
    dma = pltpu.SemaphoreType.DMA
    shared = roots == 2 and owners == 4 and n == 2 * owners
    f32, bf16 = jnp.float32, jnp.bfloat16
    if shared:
        gram = {
            "gram_sum": pltpu.VMEM((spans, spans // roots), f32),
            "strips": pltpu.VMEM((roots, width, spans // roots), LINK),
            "diag_out": pltpu.VMEM((2, SUBLANES, width), f32), "diag_in": pltpu.VMEM((n, SUBLANES, width), f32),
            "diag": pltpu.VMEM((SUBLANES, width), f32),
            "tree_out": pltpu.VMEM((5, width, spans // roots), LINK),
            "tree_in": pltpu.VMEM((5, width, spans // roots), LINK),
            "tree_send": dma((5,)), "tree_recv": dma((5,)), "diag_send": dma((2,)), "diag_recv": dma((n,)),
            "pair_send": dma((2,)), "pair_recv": dma((2,)),
        }
        rounds = 1
    else:
        gram = {
            "gram_sum": pltpu.VMEM((spans, spans), f32), "corr": pltpu.VMEM((rows, spans), f32),
            "gram_hi": pltpu.VMEM((spans, spans), bf16), "gram_lo": pltpu.VMEM((spans, spans), bf16),
        }
        rounds = PASSES
    scratch = {
        "table": pltpu.VMEM((OFFS, blk, blk), bf16), "res_v": pltpu.VMEM((rows, cols), bf16),
        "partial": pltpu.VMEM((rounds, owners, rows, width), LINK),
        "inbox": pltpu.VMEM((rounds, n, rows, width), LINK),
        "slabs": pltpu.VMEM((PASSES, owners, rows, width), bf16),
        "load_sem": dma((3,)),
        "hop_send": dma((OFFS + 3, CHUNKS)), "hop_recv": dma((OFFS, CHUNKS)),
        "swap_send": dma((OFFS, CHUNKS)), "swap_recv": dma((OFFS, CHUNKS)),
        "rs_send": dma((rounds, owners)), "rs_recv": dma((rounds, n)),
        "ag_send": dma((PASSES, n)), "ag_recv": dma((PASSES, owners)),
        **gram,
    }
    absent = dict.fromkeys(
        ("gram_hi", "gram_lo", "corr", "strips", "diag_out", "diag_in", "diag", "tree_out", "tree_in",
         "tree_send", "tree_recv", "diag_send", "diag_recv", "pair_send", "pair_recv"))

    def body(off, listed, res, sub, inv, work, sub_v, coef, *refs):
        kernel(n, roots, off, listed, res, sub, inv, work, sub_v, coef, **{**absent, **dict(zip(scratch, refs))})

    held = pl.pallas_call(
        body,
        out_shape=(
            pltpu.VMEM((rows, cols), jnp.float32),
            pltpu.VMEM((spans, cols), jnp.bfloat16),
            pltpu.VMEM((rows, spans // 2), jnp.bfloat16),
        ),
        in_specs=[smem, smem, hbm, hbm, hbm],
        out_specs=(vmem, vmem, vmem),
        scratch_shapes=list(scratch.values()),
        compiler_params=pltpu.CompilerParams(
            collective_id=0, has_side_effects=True, vmem_limit_bytes=VMEM_GRANT),
    )(owner_offset, listed, residual, subspace, inverses)
    return pl.pallas_call(
        functools.partial(finish, n, blk),
        out_shape=jax.ShapeDtypeStruct((rows, cols), jnp.float32),
        in_specs=[vmem, vmem, vmem],
        out_specs=hbm,
        scratch_shapes=[pltpu.VMEM((rows, cols), jnp.float32), dma((blocks,))],
        compiler_params=pltpu.CompilerParams(vmem_limit_bytes=16 * 2**20),
    )(*held)


def solution(mesh):
    body = functools.partial(per_device, mesh.shape["tr"], mesh.shape["root"])
    return jax.shard_map(
        body,
        mesh=mesh,
        in_specs=(
            P("root", ("grp", "tr")),
            P(None, ("grp", "tr")),
            P(("grp", "tr"), None, None),
            P(("grp", "tr")),
            P(("grp", "tr")),
        ),
        out_specs=P("root", ("grp", "tr")),
        check_vma=False,
    )
```
